256 devices in a mesh: gx: 8 (over x_hi, y), gy: 32 (over z, x_lo, core).
Axes of the slice: x: 4 (x_hi: 2, x_lo: 2; x = x_hi * 2 + x_lo), y: 4, z: 8, core: 2. Of those that a mesh axis runs over, the one named last changes fastest.
Arguments:
- image: float32 [1024, 131072], P('gx', 'gy'), may hold values from -6 to 6
- psfs: bfloat16 [32, 64, 32, 1024], P('gx', 'gy'), may hold values from -0.11035156 to 0.11035156
Outputs:
- hessian_image: float32 [1024, 131072], P('gx', 'gy')
The draws below stay inside these ranges and needn't reach their ends.
All inputs are finite; a program needn't handle non-finite values.
Results may differ from the reference program's by a relative error of at most 0.023.
Values may be sent and summed in bfloat16 or wider, within the bound.
A program may use at most 128 MiB of HBM per device.

```python
import jax
import jax.numpy as jnp
from jax import lax

PATCH = 64
PSFW = 32
DEPTH = 64
FFTL = 96
NX = 1024
NY = 2048
GX = 32
GY = 64


def levels(own_key, extent, split, smallest, high):
    def one(dim, shards_of):
        steps = jax.random.uniform(jax.random.fold_in(jax.random.fold_in(own_key, 6), dim), (shards_of,), jnp.float32, smallest / len(split), high / len(split))
        return jnp.repeat(jnp.exp(steps), extent[dim] // shards_of).reshape((-1,) + (1,) * (len(extent) - dim - 1))

    factor_of = one(*split[0])
    for cut in split[1:]:
        factor_of = factor_of * one(*cut)
    return factor_of


def gaussian(rng, extent, scale, most, cuts=(), kind=jnp.bfloat16):
    factor_of = levels(rng, extent, cuts, -0.22, 0.18) if cuts else 1.0
    values = jax.random.normal(rng, extent, jnp.float32) * scale * factor_of
    return jnp.minimum(jnp.maximum(values, -most), most).astype(kind)


def setup_inputs(seed: int = 0) -> dict:
    splits = jax.random.split(jax.random.key(seed), 3)
    image = gaussian(splits[0], (NX, NY * DEPTH), 1.0, 6.0, ((0, 8), (1, 32)), jnp.float32)
    psfs = gaussian(splits[1], (GX, GY, PSFW, PSFW * PSFW), (3.2 / PSFW ** 1.5), 0.11035156, ((0, 8), (1, 32)))
    return dict(image=image, psfs=psfs)


BLEND = (0.125, 0.375, 0.375, 0.125)


def rounded(values):
    real_part = jnp.real(values).astype(jnp.bfloat16)
    imag_part = jnp.imag(values).astype(jnp.bfloat16)
    real_part, imag_part = lax.optimization_barrier((real_part, imag_part))
    return real_part.astype(jnp.float32) + 1j * imag_part.astype(jnp.float32)


def forward(cube):
    spectrum = rounded(jnp.fft.fft(cube, n=FFTL, axis=2))
    spectrum = rounded(jnp.fft.fft(spectrum, n=FFTL, axis=1))
    return rounded(jnp.fft.fft(spectrum, n=FFTL, axis=0))


def response(cells, psf):
    product = rounded(forward(cells) * forward(psf))
    back = rounded(jnp.fft.ifft(product, axis=0))
    back = rounded(jnp.fft.ifft(back, axis=1))
    whole = jnp.real(jnp.fft.ifft(back, axis=2))
    return whole[:, :, PSFW // 2:PSFW // 2 + DEPTH].astype(jnp.float32)


def reference(image, psfs):
    half = PSFW // 2
    field = image.reshape(NX, NY, DEPTH)
    padded_nodes = jnp.pad(psfs, ((1, 1), (1, 1), (0, 0), (0, 0)))
    weights = jnp.array(BLEND, jnp.float32)
    columns = NY // PATCH
    count = (NX // PATCH) * columns

    def step(total, index):
        row = index // columns
        column = index % columns
        zero = jnp.int32(0)
        cells = lax.dynamic_slice(field, (row * PATCH, column * PATCH, zero), (PATCH, PATCH, DEPTH))
        cells = lax.optimization_barrier(cells.astype(jnp.bfloat16)).astype(jnp.float32)
        window = lax.dynamic_slice(padded_nodes, (2 * row, 2 * column, zero, zero), (4, 4, PSFW, PSFW * PSFW))
        blended = jnp.einsum('a,b,abcd->cd', weights, weights, window.astype(jnp.float32))
        blended = lax.optimization_barrier(blended.astype(jnp.bfloat16)).astype(jnp.float32)
        part = response(cells, blended.reshape(PSFW, PSFW, PSFW))
        start = (row * PATCH, column * PATCH, zero)
        current = lax.dynamic_slice(total, start, (FFTL, FFTL, DEPTH))
        return lax.dynamic_update_slice(total, current + part, start), None

    total = jnp.zeros((NX + PSFW, NY + PSFW, DEPTH), jnp.float32)
    total, _ = lax.scan(step, total, jnp.arange(count, dtype=jnp.int32))
    return total[half:half + NX, half:half + NY].reshape(NX, NY * DEPTH)
```

```python
import math

import jax
import jax.numpy as jnp
import numpy as np
from jax import lax
from jax.experimental import pallas as pl
from jax.experimental.pallas import tpu as pltpu
from jax.sharding import PartitionSpec as P

PATCH = 64
PSFW = 32
DEPTH = 64
HALF = PSFW // 2
LXY = PATCH + PSFW
LZ = DEPTH + HALF
BINS = LXY // 2
PATCHES = 2
LANES = 128
TILE = PATCHES * PATCH
EXT = TILE + PSFW
SY = 2 * PATCH + 4
SP = 2 * PSFW + 4
SZ = 2 * LZ + 4
COLS = LXY * DEPTH
BLEND = (0.125, 0.375, 0.375, 0.125)
CORNER = BLEND[0] * BLEND[0]
PIECES = ((0, 1), (1, 1), (0, 1), (1, 1), (0, 1), (1, 1), (0, CORNER), (0, CORNER), (1, CORNER), (1, CORNER))
BAND = HALF * DEPTH
INNER = PATCH * DEPTH
MESH = pl.DeviceIdType.MESH
F32 = jnp.float32
BF16 = jnp.bfloat16


def tables():
    theta = 2.0 * math.pi * (np.arange(BINS) + 0.5) / LXY

    fx = np.zeros((2, LANES, PATCHES, PATCH))
    ang = theta[:, None] * np.arange(PATCH)[None, :]
    for p in range(PATCHES):
        fx[0, p * BINS:(p + 1) * BINS, p] = np.cos(ang)
        fx[1, p * BINS:(p + 1) * BINS, p] = -np.sin(ang)
    fx = fx.reshape(2 * LANES, TILE)

    ang = theta[:, None] * np.arange(PSFW)[None, :]
    bare = np.stack([np.cos(ang), -np.sin(ang)])
    own = np.zeros((2, LANES, 2 * PATCHES, 2, PSFW))
    for p in range(PATCHES):
        for a in range(4):
            row = 2 * p + a - 1
            if 0 <= row < 2 * PATCHES:
                for col in range(2):
                    own[:, p * BINS:(p + 1) * BINS, row, col] = BLEND[a] * BLEND[col + 1] * bare
    own = own.reshape(2 * LANES, -1)
    halo = np.zeros((2, LANES, len(PIECES), PSFW))
    for i, (p, weight) in enumerate(PIECES):
        halo[:, p * BINS:(p + 1) * BINS, i] = weight * bare
    halo = halo.reshape(2 * LANES, -1)

    def pair(cos, sin, sign):
        return np.stack([np.stack([cos, -sign * sin]), np.stack([sign * sin, cos])])

    def depth(count, depths):
        ang = 2.0 * math.pi / LZ * np.outer(np.arange(LZ), np.arange(depths))
        quad = pair(np.cos(ang), np.sin(ang), -1.0)
        out = np.zeros((2, count, LZ, 2, count, depths))
        for y in range(count):
            out[:, y, :, :, y, :] = quad.transpose(0, 2, 1, 3)
        return out.reshape(2 * count * LZ, 2 * count * depths)

    gz = depth(2, DEPTH)
    gzp = depth(4, PSFW)

    def flat(quad):
        o, i, r, c = quad.shape
        return quad.transpose(0, 2, 1, 3).reshape(o * r, i * c)

    ang = 2.0 * math.pi / LXY * np.outer(np.arange(LXY), np.arange(LXY))
    full = pair(np.cos(ang), np.sin(ang), -1.0)
    fy = flat(full[:, :, :, :PATCH])
    fyp = flat(full[:, :, :, :PSFW])
    gy = flat(pair(np.cos(ang), np.sin(ang), 1.0)) / LXY

    ang = 2.0 * math.pi / LZ * np.outer(np.arange(DEPTH) + HALF, np.arange(LZ))
    iz = flat(pair(np.cos(ang), np.sin(ang), 1.0)) / LZ

    ix = np.zeros((EXT, 2, LANES))
    ang = np.arange(LXY)[:, None] * theta[None, :]
    for p in range(PATCHES):
        ix[p * PATCH:p * PATCH + LXY, 0, p * BINS:(p + 1) * BINS] = np.cos(ang) * 2.0 / LXY
        ix[p * PATCH:p * PATCH + LXY, 1, p * BINS:(p + 1) * BINS] = -np.sin(ang) * 2.0 / LXY
    ix = ix.reshape(EXT, 2 * LANES)

    return [jnp.asarray(t, BF16) for t in [fx, gz, gzp, fy, fyp, gy, iz, ix, own, halo]]


def mm(a, b):
    return lax.dot_general(a, b, (((1,), (0,)), ((), ())), preferred_element_type=F32)


def mm_t(a, b):
    return lax.dot_general(a, b, (((1,), (1,)), ((), ())), preferred_element_type=F32)


SIDES = ((0, -1), (0, 1), (-1, 0), (1, 0), (-1, -1), (-1, 1), (1, -1), (1, 1))
LEFT, RIGHT, UP, DOWN, UL, UR, DL, DR = range(8)
BACK = (RIGHT, LEFT, DOWN, UP, DR, DL, UR, UL)
HALO = ((0, 64), (64, 64), (128, 32), (160, 32), (192, 32), (224, 32), (256, 32), (288, 32))
NODE = PSFW
GROUPS = LXY // 4
U_DEPTH, U_IMAGE, U_PSF, U_BACK, U_INNER = 4, 4, 2, 4, 4
EDGE = HALF // 4


def kernel(image, psfs, fx, gz, gzp, fy, fyp, gy, iz, ix, pown, phalo,
           result,
           img, own, part, halo, d1, e1, spec, pspec, ispec, resp, out,
           ysend, xsend, yrecv, xrecv, crecv,
           image_sem, own_sem, out_sem, psend_sem, precv_sem, rsend_sem, rrecv_sem):
    gx, gy_ = lax.axis_index("gx"), lax.axis_index("gy")
    last_x, last_y = lax.axis_size("gx") - 1, lax.axis_size("gy") - 1

    def present(side):
        dx, dy = SIDES[side]
        terms = []
        if dx:
            terms.append(gx > 0 if dx < 0 else gx < last_x)
        if dy:
            terms.append(gy_ > 0 if dy < 0 else gy_ < last_y)
        return terms[0] if len(terms) == 1 else jnp.logical_and(terms[0], terms[1])

    def place(side):
        dx, dy = SIDES[side]
        return (gx + dx, gy_ + dy)

    own_copy = pltpu.make_async_copy(psfs, own, own_sem)
    own_copy.start()
    chunk = INNER // 4
    image_copies = []
    for t in range(4):
        sl = pl.ds(t * chunk, chunk)
        image_copies.append(pltpu.make_async_copy(image.at[:, sl], img.at[:, sl], image_sem.at[t]))
        image_copies[-1].start()

    barrier = pltpu.get_barrier_semaphore()
    count = jnp.int32(0)
    for side in range(8):
        count = count + present(side).astype(jnp.int32)

        @pl.when(present(side))
        def _():
            pl.semaphore_signal(barrier, inc=1, device_id=place(side), device_id_type=MESH)

    own_copy.wait()

    def node(r, c):
        row = (r * 2 + c) * NODE
        return own[row:row + NODE, :].astype(F32)

    def put(row, value):
        part[row:row + NODE, :] = value.astype(BF16)

    w0, w1 = BLEND[0], BLEND[1]
    for col, at in ((0, 0), (1, 64)):
        n0, n1, n2, n3 = (node(r, col) for r in range(4))
        put(at, (w0 * w1) * (n0 + n1) + (w0 * w0) * n2)
        put(at + NODE, (w0 * w0) * n1 + (w0 * w1) * (n2 + n3))
    put(128, (w0 * w1) * (node(0, 0) + node(0, 1)))
    put(160, (w0 * w1) * (node(3, 0) + node(3, 1)))
    corner = {UL: 0, UR: 1, DL: 6, DR: 7}

    def psf_copy(side, target=None):
        if side in corner:
            src = own.at[pl.ds(corner[side] * NODE, NODE), :]
        else:
            src = part.at[pl.ds(*HALO[side]), :]
        return pltpu.make_async_remote_copy(
            src_ref=src, dst_ref=halo.at[pl.ds(*HALO[BACK[side]]), :],
            send_sem=psend_sem.at[side], recv_sem=precv_sem.at[BACK[side]],
            device_id=place(side if target is None else target), device_id_type=MESH)

    pl.semaphore_wait(barrier, count)
    for side in range(8):
        @pl.when(present(side))
        def _():
            psf_copy(side).start()

        @pl.when(jnp.logical_not(present(side)))
        def _():
            halo[pl.ds(*HALO[side]), :] = jnp.zeros((HALO[side][1], PSFW * PSFW), BF16)

    width = 512
    for t in range(INNER // width):
        if t % (chunk // width) == 0:
            image_copies[t // (chunk // width)].wait()
        sl = slice(t * width, (t + 1) * width)
        d1[:, sl] = mm(fx[...], img[:, sl].astype(BF16)).astype(BF16)

    def depth_step(ref, table, t, ylo, width_y, stride, out):
        def rhs(tile):
            sl = pl.ds(pl.multiple_of(tile * LANES, LANES), LANES)
            return jnp.concatenate([ref[:LANES, sl], ref[LANES:, sl]], axis=1)

        both = jnp.concatenate([rhs(2 * t), rhs(2 * t + 1)], axis=0)
        res = mm_t(table[...], both)
        for jj in range(2):
            for part in range(2):
                for y in range(ylo):
                    row = (part * ylo + y) * LZ
                    block = res[row:row + LZ, jj * LANES:(jj + 1) * LANES]
                    start = part * width_y + (2 * t + jj) * ylo + y
                    out[pl.ds(start, LZ, stride=stride), :] = block

    @pl.loop(0, 16, unroll=U_DEPTH)
    def _(t):
        depth_step(d1, gz, t, 2, PATCH, SY, spec)

    def slab(ref, t, rows, stride):
        parts = [ref[pl.ds((2 * t + h) * stride, rows), :] for h in range(2)]
        return jnp.concatenate(parts, axis=1).astype(BF16)

    @pl.loop(0, LZ // 2, unroll=U_IMAGE)
    def _(t):
        ispec[t] = mm(fy[...], slab(spec, t, 2 * PATCH, SY)).astype(BF16)

    for side in range(8):
        @pl.when(present(side))
        def _():
            psf_copy(BACK[side], side).wait_recv()
    for t in range(2):
        sl = slice(t * 512, (t + 1) * 512)
        e1[:, sl] = (mm(pown[...], own[:, sl]) + mm(phalo[...], halo[:, sl])).astype(BF16)

    @pl.loop(0, 4, unroll=U_PSF)
    def _(t):
        depth_step(e1, gzp, t, 4, PSFW, SP, pspec)

    @pl.loop(0, LZ // 2, unroll=U_BACK)
    def _(t):
        b = mm(fyp[...], slab(pspec, t, 2 * PSFW, SP))
        a = ispec[t].astype(F32)
        ar, ai, br, bi = a[:LXY], a[LXY:], b[:LXY], b[LXY:]
        prod = jnp.concatenate([ar * br - ai * bi, ar * bi + ai * br], axis=0).astype(BF16)
        back = mm(gy[...], prod)
        for h in range(2):
            for part_ in range(2):
                block = back[part_ * LXY:(part_ + 1) * LXY, h * LANES:(h + 1) * LANES]
                resp[pl.ds(part_ * LZ + 2 * t + h, LXY, stride=SZ), :] = block

    def group(g):
        rows = []
        for h in range(2):
            parts = [resp[pl.ds((4 * g + 2 * h + q) * SZ, 2 * LZ), :] for q in range(2)]
            flat = jnp.concatenate(parts, axis=1).astype(BF16)
            z = mm(iz[...], flat).astype(BF16)
            for q in range(2):
                half = z[:, q * LANES:(q + 1) * LANES]
                rows.append(jnp.concatenate([half[:DEPTH], half[DEPTH:]], axis=1))
        return mm_t(ix[...], jnp.concatenate(rows, axis=0))

    for side in range(2):
        @pl.loop(0, EDGE, unroll=EDGE)
        def _(e):
            cols = pl.ds(pl.multiple_of(e * 256, 256), 256)
            ysend[side, :, cols] = group(e + side * (GROUPS - EDGE)).astype(BF16)

    def y_copy(side, target):
        dx, dy = SIDES[side]
        rows = {0: pl.ds(HALF, TILE), -1: pl.ds(0, HALF), 1: pl.ds(HALF + TILE, HALF)}[dx]
        dst = yrecv.at[BACK[side]] if dx == 0 else crecv.at[BACK[side] - 4]
        return pltpu.make_async_remote_copy(
            src_ref=ysend.at[side if dx == 0 else (dy + 1) // 2, rows, :], dst_ref=dst,
            send_sem=rsend_sem.at[side], recv_sem=rrecv_sem.at[BACK[side]],
            device_id=place(side if target is None else target), device_id_type=MESH)

    def x_copy(side, target):
        return pltpu.make_async_remote_copy(
            src_ref=xsend.at[side - 2], dst_ref=xrecv.at[BACK[side] - 2],
            send_sem=rsend_sem.at[side], recv_sem=rrecv_sem.at[BACK[side]],
            device_id=place(side if target is None else target), device_id_type=MESH)

    def response_copy(side, target=None):
        return (x_copy if side in (UP, DOWN) else y_copy)(side, target)

    for side in (LEFT, RIGHT, UL, UR, DL, DR):
        @pl.when(present(side))
        def _():
            response_copy(side).start()

    @pl.loop(0, GROUPS - 2 * EDGE, unroll=U_INNER)
    def _(g):
        cols = pl.ds(pl.multiple_of(g * 256, 256), 256)
        value = group(g + EDGE)
        out[:, cols] = value[HALF:HALF + TILE]
        xsend[0, :, cols] = value[:HALF].astype(BF16)
        xsend[1, :, cols] = value[HALF + TILE:].astype(BF16)

    for side in (UP, DOWN):
        @pl.when(present(side))
        def _():
            response_copy(side).start()

    def arrive(side, rows, cols, ref):
        @pl.when(present(side))
        def _():
            response_copy(BACK[side], side).wait_recv()
            out[rows, cols] += ref[...].astype(F32)

    top, bottom = pl.ds(0, HALF), pl.ds(TILE - HALF, HALF)
    first, last = pl.ds(0, BAND), pl.ds(INNER - BAND, BAND)
    every = pl.ds(0, TILE)
    arrive(UP, top, pl.ds(0, INNER), xrecv.at[0])
    arrive(DOWN, bottom, pl.ds(0, INNER), xrecv.at[1])
    middle = pltpu.make_async_copy(
        out.at[:, pl.ds(BAND, INNER - 2 * BAND)], result.at[:, pl.ds(BAND, INNER - 2 * BAND)], out_sem.at[0])
    middle.start()
    arrive(UL, top, first, crecv.at[0])
    arrive(DL, bottom, first, crecv.at[2])
    arrive(LEFT, every, first, yrecv.at[0])
    one = pltpu.make_async_copy(out.at[:, first], result.at[:, first], out_sem.at[1])
    one.start()
    arrive(UR, top, last, crecv.at[1])
    arrive(DR, bottom, last, crecv.at[3])
    arrive(RIGHT, every, last, yrecv.at[1])
    two = pltpu.make_async_copy(out.at[:, last], result.at[:, last], out_sem.at[2])
    two.start()

    for side in range(8):
        @pl.when(present(side))
        def _():
            psf_copy(side).wait_send()
            response_copy(side).wait_send()
    middle.wait()
    one.wait()
    two.wait()


def compute(image, psfs, *consts):
    vmem, anywhere = pl.BlockSpec(memory_space=pltpu.VMEM), pl.BlockSpec(memory_space=pl.ANY)
    dma = pltpu.SemaphoreType.DMA
    return pl.pallas_call(
        kernel,
        out_shape=jax.ShapeDtypeStruct((TILE, INNER), F32),
        in_specs=[anywhere, anywhere] + [vmem] * len(consts),
        out_specs=anywhere,
        scratch_shapes=[
            pltpu.VMEM((TILE, INNER), F32),
            pltpu.VMEM((8 * PSFW, PSFW * PSFW), BF16),
            pltpu.VMEM((6 * PSFW, PSFW * PSFW), BF16),
            pltpu.VMEM((10 * PSFW, PSFW * PSFW), BF16),
            pltpu.VMEM((2 * LANES, INNER), BF16),
            pltpu.VMEM((2 * LANES, PSFW * PSFW), BF16),
            pltpu.VMEM((LZ * SY, LANES), F32),
            pltpu.VMEM((LZ * SP, LANES), F32),
            pltpu.VMEM((LZ // 2, 2 * LXY, 2 * LANES), BF16),
            pltpu.VMEM((LXY * SZ, LANES), F32),
            pltpu.VMEM((TILE, INNER), F32),
            pltpu.VMEM((2, EXT, BAND), BF16),
            pltpu.VMEM((2, HALF, INNER), BF16),
            pltpu.VMEM((2, TILE, BAND), BF16),
            pltpu.VMEM((2, HALF, INNER), BF16),
            pltpu.VMEM((4, HALF, BAND), BF16),
            dma((4,)), dma, dma((3,)), dma((8,)), dma((8,)), dma((8,)), dma((8,)),
        ],
        compiler_params=pltpu.CompilerParams(
            vmem_limit_bytes=60 * 1024 * 1024, collective_id=0, has_side_effects=True),
    )(image, psfs.reshape(8 * PSFW, PSFW * PSFW), *consts)


def body(image, psfs):
    return compute(image, psfs, *tables())


def solution(mesh):
    placed = (P("gx", "gy"), P("gx", "gy", None, None))
    return jax.shard_map(body, mesh=mesh, in_specs=placed, out_specs=P("gx", "gy"), check_vma=False)
```

```python
import math

import jax
import jax.numpy as jnp
import numpy as np
from jax import lax
from jax.experimental import pallas as pl
from jax.experimental.pallas import tpu as pltpu
from jax.sharding import PartitionSpec as P

PATCH = 64
PSFW = 32
DEPTH = 64
HALF = PSFW // 2
LXY = PATCH + PSFW
LZ = DEPTH + HALF
BINS = LXY // 2
PATCHES = 2
LANES = 128
TILE = PATCHES * PATCH
EXT = TILE + PSFW
SY = 2 * PATCH + 4
SP = 2 * PSFW + 4
SZ = 2 * LZ + 4
COLS = LXY * DEPTH
BLEND = (0.125, 0.375, 0.375, 0.125)
CORNER = BLEND[0] * BLEND[0]
PIECES = ((0, 1), (1, 1), (0, 1), (1, 1), (0, 1), (1, 1), (0, CORNER), (0, CORNER), (1, CORNER), (1, CORNER))
BAND = HALF * DEPTH
INNER = PATCH * DEPTH
MESH = pl.DeviceIdType.MESH
F32 = jnp.float32
BF16 = jnp.bfloat16


def tables():
    theta = 2.0 * math.pi * (np.arange(BINS) + 0.5) / LXY

    fx = np.zeros((2, LANES, PATCHES, PATCH))
    ang = theta[:, None] * np.arange(PATCH)[None, :]
    for p in range(PATCHES):
        fx[0, p * BINS:(p + 1) * BINS, p] = np.cos(ang)
        fx[1, p * BINS:(p + 1) * BINS, p] = -np.sin(ang)
    fx = fx.reshape(2 * LANES, TILE)

    ang = theta[:, None] * np.arange(PSFW)[None, :]
    bare = np.stack([np.cos(ang), -np.sin(ang)])
    own = np.zeros((2, LANES, 2 * PATCHES, 2, PSFW))
    for p in range(PATCHES):
        for a in range(4):
            row = 2 * p + a - 1
            if 0 <= row < 2 * PATCHES:
                for col in range(2):
                    own[:, p * BINS:(p + 1) * BINS, row, col] = BLEND[a] * BLEND[col + 1] * bare
    own = own.reshape(2 * LANES, -1)
    halo = np.zeros((2, LANES, len(PIECES), PSFW))
    for i, (p, weight) in enumerate(PIECES):
        halo[:, p * BINS:(p + 1) * BINS, i] = weight * bare
    halo = halo.reshape(2 * LANES, -1)

    def pair(cos, sin, sign):
        return np.stack([np.stack([cos, -sign * sin]), np.stack([sign * sin, cos])])

    def depth(count, depths):
        ang = 2.0 * math.pi / LZ * np.outer(np.arange(LZ), np.arange(depths))
        quad = pair(np.cos(ang), np.sin(ang), -1.0)
        out = np.zeros((2, count, LZ, 2, count, depths))
        for y in range(count):
            out[:, y, :, :, y, :] = quad.transpose(0, 2, 1, 3)
        return out.reshape(2 * count * LZ, 2 * count * depths)

    gz = depth(2, DEPTH)
    gzp = depth(4, PSFW)

    def flat(quad):
        o, i, r, c = quad.shape
        return quad.transpose(0, 2, 1, 3).reshape(o * r, i * c)

    ang = 2.0 * math.pi / LXY * np.outer(np.arange(LXY), np.arange(LXY))
    full = pair(np.cos(ang), np.sin(ang), -1.0)
    fy = flat(full[:, :, :, :PATCH])
    fyp = flat(full[:, :, :, :PSFW])
    gy = flat(pair(np.cos(ang), np.sin(ang), 1.0)) / LXY

    ang = 2.0 * math.pi / LZ * np.outer(np.arange(DEPTH) + HALF, np.arange(LZ))
    iz = flat(pair(np.cos(ang), np.sin(ang), 1.0)) / LZ

    ix = np.zeros((EXT, 2, LANES))
    ang = np.arange(LXY)[:, None] * theta[None, :]
    for p in range(PATCHES):
        ix[p * PATCH:p * PATCH + LXY, 0, p * BINS:(p + 1) * BINS] = np.cos(ang) * 2.0 / LXY
        ix[p * PATCH:p * PATCH + LXY, 1, p * BINS:(p + 1) * BINS] = -np.sin(ang) * 2.0 / LXY
    ix = ix.reshape(EXT, 2 * LANES)

    return [jnp.asarray(t, BF16) for t in [fx, gz, gzp, fy, fyp, gy, iz, ix, own, halo]]


def mm(a, b):
    return lax.dot_general(a, b, (((1,), (0,)), ((), ())), preferred_element_type=F32)


def mm_t(a, b):
    return lax.dot_general(a, b, (((1,), (1,)), ((), ())), preferred_element_type=F32)


SIDES = ((0, -1), (0, 1), (-1, 0), (1, 0), (-1, -1), (-1, 1), (1, -1), (1, 1))
LEFT, RIGHT, UP, DOWN, UL, UR, DL, DR = range(8)
BACK = (RIGHT, LEFT, DOWN, UP, DR, DL, UR, UL)
HALO = ((0, 64), (64, 64), (128, 32), (160, 32), (192, 32), (224, 32), (256, 32), (288, 32))
NODE = PSFW
GROUPS = LXY // 4
U_DEPTH, U_IMAGE, U_PSF, U_BACK, U_INNER = 16, 40, 4, 40, 16
EDGE = HALF // 4


def kernel(image, psfs, fx, gz, gzp, fy, fyp, gy, iz, ix, pown, phalo,
           out,
           img, own, part, halo, d1, e1, spec, pspec, ispec, resp,
           ysend, xsend, yrecv, xrecv, crecv,
           image_sem, own_sem, psend_sem, precv_sem, rsend_sem, rrecv_sem):
    gx, gy_ = lax.axis_index("gx"), lax.axis_index("gy")
    last_x, last_y = lax.axis_size("gx") - 1, lax.axis_size("gy") - 1

    def present(side):
        dx, dy = SIDES[side]
        terms = []
        if dx:
            terms.append(gx > 0 if dx < 0 else gx < last_x)
        if dy:
            terms.append(gy_ > 0 if dy < 0 else gy_ < last_y)
        return terms[0] if len(terms) == 1 else jnp.logical_and(terms[0], terms[1])

    def place(side):
        dx, dy = SIDES[side]
        return (gx + dx, gy_ + dy)

    own_copy = pltpu.make_async_copy(psfs, own, own_sem)
    own_copy.start()
    chunk = INNER // 4
    image_copies = []
    for t in range(4):
        sl = pl.ds(t * chunk, chunk)
        image_copies.append(pltpu.make_async_copy(image.at[:, sl], img.at[:, sl], image_sem.at[t]))
        image_copies[-1].start()

    barrier = pltpu.get_barrier_semaphore()
    count = jnp.int32(0)
    for side in range(8):
        count = count + present(side).astype(jnp.int32)

        @pl.when(present(side))
        def _():
            pl.semaphore_signal(barrier, inc=1, device_id=place(side), device_id_type=MESH)

    own_copy.wait()

    def node(r, c):
        row = (r * 2 + c) * NODE
        return own[row:row + NODE, :].astype(F32)

    def put(row, value):
        part[row:row + NODE, :] = value.astype(BF16)

    w0, w1 = BLEND[0], BLEND[1]
    for col, at in ((0, 0), (1, 64)):
        n0, n1, n2, n3 = (node(r, col) for r in range(4))
        put(at, (w0 * w1) * (n0 + n1) + (w0 * w0) * n2)
        put(at + NODE, (w0 * w0) * n1 + (w0 * w1) * (n2 + n3))
    put(128, (w0 * w1) * (node(0, 0) + node(0, 1)))
    put(160, (w0 * w1) * (node(3, 0) + node(3, 1)))
    corner = {UL: 0, UR: 1, DL: 6, DR: 7}

    def psf_copy(side, target=None):
        if side in corner:
            src = own.at[pl.ds(corner[side] * NODE, NODE), :]
        else:
            src = part.at[pl.ds(*HALO[side]), :]
        return pltpu.make_async_remote_copy(
            src_ref=src, dst_ref=halo.at[pl.ds(*HALO[BACK[side]]), :],
            send_sem=psend_sem.at[side], recv_sem=precv_sem.at[BACK[side]],
            device_id=place(side if target is None else target), device_id_type=MESH)

    pl.semaphore_wait(barrier, count)
    for side in range(8):
        @pl.when(present(side))
        def _():
            psf_copy(side).start()

        @pl.when(jnp.logical_not(present(side)))
        def _():
            halo[pl.ds(*HALO[side]), :] = jnp.zeros((HALO[side][1], PSFW * PSFW), BF16)

    width = 512
    for t in range(INNER // width):
        if t % (chunk // width) == 0:
            image_copies[t // (chunk // width)].wait()
        sl = slice(t * width, (t + 1) * width)
        d1[:, sl] = mm(fx[...], img[:, sl].astype(BF16)).astype(BF16)

    def depth_step(ref, table, t, ylo, width_y, stride, out):
        def rhs(tile):
            sl = pl.ds(pl.multiple_of(tile * LANES, LANES), LANES)
            return jnp.concatenate([ref[:LANES, sl], ref[LANES:, sl]], axis=1)

        both = jnp.concatenate([rhs(2 * t), rhs(2 * t + 1)], axis=0)
        res = mm_t(table[...], both)
        for jj in range(2):
            for part in range(2):
                for y in range(ylo):
                    row = (part * ylo + y) * LZ
                    block = res[row:row + LZ, jj * LANES:(jj + 1) * LANES]
                    start = part * width_y + (2 * t + jj) * ylo + y
                    out[pl.ds(start, LZ, stride=stride), :] = block

    @pl.loop(0, 16, unroll=U_DEPTH)
    def _(t):
        depth_step(d1, gz, t, 2, PATCH, SY, spec)

    def slab(ref, t, rows, stride):
        parts = [ref[pl.ds((2 * t + h) * stride, rows), :] for h in range(2)]
        return jnp.concatenate(parts, axis=1).astype(BF16)

    @pl.loop(0, LZ // 2, unroll=U_IMAGE)
    def _(t):
        ispec[t] = mm(fy[...], slab(spec, t, 2 * PATCH, SY)).astype(BF16)

    for side in range(8):
        @pl.when(present(side))
        def _():
            psf_copy(BACK[side], side).wait_recv()
    for t in range(2):
        sl = slice(t * 512, (t + 1) * 512)
        e1[:, sl] = (mm(pown[...], own[:, sl]) + mm(phalo[...], halo[:, sl])).astype(BF16)

    @pl.loop(0, 4, unroll=U_PSF)
    def _(t):
        depth_step(e1, gzp, t, 4, PSFW, SP, pspec)

    @pl.loop(0, LZ // 2, unroll=U_BACK)
    def _(t):
        b = mm(fyp[...], slab(pspec, t, 2 * PSFW, SP)).astype(BF16)
        a = ispec[t]
        ar, ai, br, bi = a[:LXY], a[LXY:], b[:LXY], b[LXY:]
        prod = jnp.concatenate([ar * br - ai * bi, ar * bi + ai * br], axis=0)
        back = mm(gy[...], prod)
        for h in range(2):
            for part_ in range(2):
                block = back[part_ * LXY:(part_ + 1) * LXY, h * LANES:(h + 1) * LANES]
                resp[pl.ds(part_ * LZ + 2 * t + h, LXY, stride=SZ), :] = block

    def group(g):
        rows = []
        for h in range(2):
            parts = [resp[pl.ds((4 * g + 2 * h + q) * SZ, 2 * LZ), :] for q in range(2)]
            flat = jnp.concatenate(parts, axis=1).astype(BF16)
            z = mm(iz[...], flat).astype(BF16)
            for q in range(2):
                half = z[:, q * LANES:(q + 1) * LANES]
                rows.append(jnp.concatenate([half[:DEPTH], half[DEPTH:]], axis=1))
        return mm_t(ix[...], jnp.concatenate(rows, axis=0))

    for side in range(2):
        @pl.loop(0, EDGE, unroll=EDGE)
        def _(e):
            cols = pl.ds(pl.multiple_of(e * 256, 256), 256)
            ysend[side, :, cols] = group(e + side * (GROUPS - EDGE)).astype(BF16)

    def y_copy(side, target):
        dx, dy = SIDES[side]
        rows = {0: pl.ds(HALF, TILE), -1: pl.ds(0, HALF), 1: pl.ds(HALF + TILE, HALF)}[dx]
        dst = yrecv.at[BACK[side]] if dx == 0 else crecv.at[BACK[side] - 4]
        return pltpu.make_async_remote_copy(
            src_ref=ysend.at[side if dx == 0 else (dy + 1) // 2, rows, :], dst_ref=dst,
            send_sem=rsend_sem.at[side], recv_sem=rrecv_sem.at[BACK[side]],
            device_id=place(side if target is None else target), device_id_type=MESH)

    def x_copy(side, target):
        return pltpu.make_async_remote_copy(
            src_ref=xsend.at[side - 2], dst_ref=xrecv.at[BACK[side] - 2],
            send_sem=rsend_sem.at[side], recv_sem=rrecv_sem.at[BACK[side]],
            device_id=place(side if target is None else target), device_id_type=MESH)

    def response_copy(side, target=None):
        return (x_copy if side in (UP, DOWN) else y_copy)(side, target)

    for side in (LEFT, RIGHT, UL, UR, DL, DR):
        @pl.when(present(side))
        def _():
            response_copy(side).start()

    @pl.loop(0, GROUPS - 2 * EDGE, unroll=U_INNER)
    def _(g):
        cols = pl.ds(pl.multiple_of(g * 256, 256), 256)
        value = group(g + EDGE)
        out[:, cols] = value[HALF:HALF + TILE]
        xsend[0, :, cols] = value[:HALF].astype(BF16)
        xsend[1, :, cols] = value[HALF + TILE:].astype(BF16)

    for side in (UP, DOWN):
        @pl.when(present(side))
        def _():
            response_copy(side).start()

    def arrive(side, rows, cols, ref):
        @pl.when(present(side))
        def _():
            response_copy(BACK[side], side).wait_recv()
            out[rows, cols] += ref[...].astype(F32)

    top, bottom = pl.ds(0, HALF), pl.ds(TILE - HALF, HALF)
    first, last = pl.ds(0, BAND), pl.ds(INNER - BAND, BAND)
    every = pl.ds(0, TILE)
    arrive(UP, top, pl.ds(0, INNER), xrecv.at[0])
    arrive(DOWN, bottom, pl.ds(0, INNER), xrecv.at[1])
    arrive(UL, top, first, crecv.at[0])
    arrive(DL, bottom, first, crecv.at[2])
    arrive(LEFT, every, first, yrecv.at[0])
    arrive(UR, top, last, crecv.at[1])
    arrive(DR, bottom, last, crecv.at[3])
    arrive(RIGHT, every, last, yrecv.at[1])
    for side in range(8):
        @pl.when(present(side))
        def _():
            psf_copy(side).wait_send()
            response_copy(side).wait_send()


def compute(image, psfs, *consts):
    vmem, anywhere = pl.BlockSpec(memory_space=pltpu.VMEM), pl.BlockSpec(memory_space=pltpu.HBM)
    dma = pltpu.SemaphoreType.DMA
    return pl.pallas_call(
        kernel,
        out_shape=jax.ShapeDtypeStruct((TILE, INNER), F32),
        in_specs=[anywhere, anywhere] + [vmem] * len(consts),
        out_specs=vmem,
        scratch_shapes=[
            pltpu.VMEM((TILE, INNER), F32),
            pltpu.VMEM((8 * PSFW, PSFW * PSFW), BF16),
            pltpu.VMEM((6 * PSFW, PSFW * PSFW), BF16),
            pltpu.VMEM((10 * PSFW, PSFW * PSFW), BF16),
            pltpu.VMEM((2 * LANES, INNER), BF16),
            pltpu.VMEM((2 * LANES, PSFW * PSFW), BF16),
            pltpu.VMEM((LZ * SY, LANES), F32),
            pltpu.VMEM((LZ * SP, LANES), F32),
            pltpu.VMEM((LZ // 2, 2 * LXY, 2 * LANES), BF16),
            pltpu.VMEM((LXY * SZ, LANES), F32),
            pltpu.VMEM((2, EXT, BAND), BF16),
            pltpu.VMEM((2, HALF, INNER), BF16),
            pltpu.VMEM((2, TILE, BAND), BF16),
            pltpu.VMEM((2, HALF, INNER), BF16),
            pltpu.VMEM((4, HALF, BAND), BF16),
            dma((4,)), dma, dma((8,)), dma((8,)), dma((8,)), dma((8,)),
        ],
        compiler_params=pltpu.CompilerParams(
            vmem_limit_bytes=49 * 1024 * 1024, collective_id=0, has_side_effects=True),
    )(image, psfs.reshape(8 * PSFW, PSFW * PSFW), *consts)


def body(image, psfs):
    return compute(image, psfs, *tables())


def solution(mesh):
    placed = (P("gx", "gy"), P("gx", "gy", None, None))
    return jax.shard_map(body, mesh=mesh, in_specs=placed, out_specs=P("gx", "gy"), check_vma=False)
```

```python
import math

import jax
import jax.numpy as jnp
import numpy as np
from jax import lax
from jax.experimental import pallas as pl
from jax.experimental.pallas import tpu as pltpu
from jax.sharding import PartitionSpec as P

PATCH = 64
PSFW = 32
DEPTH = 64
HALF = PSFW // 2
LXY = PATCH + PSFW
LZ = DEPTH + HALF
BINS = LXY // 2
PATCHES = 2
LANES = 128
TILE = PATCHES * PATCH
EXT = TILE + PSFW
SY = 2 * PATCH + 4
SP = 2 * PSFW + 4
SZ = 2 * LZ + 4
COLS = LXY * DEPTH
BLEND = (0.125, 0.375, 0.375, 0.125)
CORNER = BLEND[0] * BLEND[0]
PIECES = ((0, 1), (1, 1), (0, 1), (1, 1), (0, 1), (1, 1), (0, CORNER), (0, CORNER), (1, CORNER), (1, CORNER))
BAND = HALF * DEPTH
INNER = PATCH * DEPTH
MESH = pl.DeviceIdType.MESH
F32 = jnp.float32
BF16 = jnp.bfloat16


def tables():
    theta = 2.0 * math.pi * (np.arange(BINS) + 0.5) / LXY

    fx = np.zeros((2, LANES, PATCHES, PATCH))
    ang = theta[:, None] * np.arange(PATCH)[None, :]
    for p in range(PATCHES):
        fx[0, p * BINS:(p + 1) * BINS, p] = np.cos(ang)
        fx[1, p * BINS:(p + 1) * BINS, p] = -np.sin(ang)
    fx = fx.reshape(2 * LANES, TILE)

    ang = theta[:, None] * np.arange(PSFW)[None, :]
    bare = np.stack([np.cos(ang), -np.sin(ang)])
    own = np.zeros((2, LANES, 2 * PATCHES, 2, PSFW))
    for p in range(PATCHES):
        for a in range(4):
            row = 2 * p + a - 1
            if 0 <= row < 2 * PATCHES:
                for col in range(2):
                    own[:, p * BINS:(p + 1) * BINS, row, col] = BLEND[a] * BLEND[col + 1] * bare
    own = own.reshape(2 * LANES, -1)
    halo = np.zeros((2, LANES, len(PIECES), PSFW))
    for i, (p, weight) in enumerate(PIECES):
        halo[:, p * BINS:(p + 1) * BINS, i] = weight * bare
    halo = halo.reshape(2 * LANES, -1)

    def pair(cos, sin, sign):
        return np.stack([np.stack([cos, -sign * sin]), np.stack([sign * sin, cos])])

    def depth(count, depths):
        ang = 2.0 * math.pi / LZ * np.outer(np.arange(LZ), np.arange(depths))
        quad = pair(np.cos(ang), np.sin(ang), -1.0)
        out = np.zeros((2, count, LZ, 2, count, depths))
        for y in range(count):
            out[:, y, :, :, y, :] = quad.transpose(0, 2, 1, 3)
        return out.reshape(2 * count * LZ, 2 * count * depths)

    gz = depth(2, DEPTH)
    gzp = depth(4, PSFW)

    def flat(quad):
        o, i, r, c = quad.shape
        return quad.transpose(0, 2, 1, 3).reshape(o * r, i * c)

    ang = 2.0 * math.pi / LXY * np.outer(np.arange(LXY), np.arange(LXY))
    full = pair(np.cos(ang), np.sin(ang), -1.0)
    fy = flat(full[:, :, :, :PATCH])
    fyp = flat(full[:, :, :, :PSFW])
    gy = flat(pair(np.cos(ang), np.sin(ang), 1.0)) / LXY

    ang = 2.0 * math.pi / LZ * np.outer(np.arange(DEPTH) + HALF, np.arange(LZ))
    iz = flat(pair(np.cos(ang), np.sin(ang), 1.0)) / LZ

    ix = np.zeros((EXT, 2, LANES))
    ang = np.arange(LXY)[:, None] * theta[None, :]
    for p in range(PATCHES):
        ix[p * PATCH:p * PATCH + LXY, 0, p * BINS:(p + 1) * BINS] = np.cos(ang) * 2.0 / LXY
        ix[p * PATCH:p * PATCH + LXY, 1, p * BINS:(p + 1) * BINS] = -np.sin(ang) * 2.0 / LXY
    ix = ix.reshape(EXT, 2 * LANES)

    return [jnp.asarray(t, BF16) for t in [fx, gz, gzp, fy, fyp, gy, iz, ix, own, halo]]


def mm(a, b):
    return lax.dot_general(a, b, (((1,), (0,)), ((), ())), preferred_element_type=F32)


def mm_t(a, b):
    return lax.dot_general(a, b, (((1,), (1,)), ((), ())), preferred_element_type=F32)


SIDES = ((0, -1), (0, 1), (-1, 0), (1, 0), (-1, -1), (-1, 1), (1, -1), (1, 1))
LEFT, RIGHT, UP, DOWN, UL, UR, DL, DR = range(8)
BACK = (RIGHT, LEFT, DOWN, UP, DR, DL, UR, UL)
HALO = ((0, 64), (64, 64), (128, 32), (160, 32), (192, 32), (224, 32), (256, 32), (288, 32))
NODE = PSFW
GROUPS = LXY // 4
U_DEPTH, U_IMAGE, U_PSF, U_BACK, U_INNER = 16, 40, 4, 40, 16
EDGE = HALF // 4


def kernel(image, psfs, *refs):
    kernel_body(image, psfs, refs[:10], *refs[10:])


def kernel_body(image, psfs, table_refs,
           out,
           img, own, part, halo, d1, e1, spec, pspec, ispec, resp,
           ysend, xsend, yrecv, xrecv, crecv,
           fx, gz, gzp, fy, fyp, gy, iz, ix, pown, phalo,
           image_sem, own_sem, table_sem, psend_sem, precv_sem, rsend_sem, rrecv_sem):
    gx, gy_ = lax.axis_index("gx"), lax.axis_index("gy")
    last_x, last_y = lax.axis_size("gx") - 1, lax.axis_size("gy") - 1

    def present(side):
        dx, dy = SIDES[side]
        terms = []
        if dx:
            terms.append(gx > 0 if dx < 0 else gx < last_x)
        if dy:
            terms.append(gy_ > 0 if dy < 0 else gy_ < last_y)
        return terms[0] if len(terms) == 1 else jnp.logical_and(terms[0], terms[1])

    def place(side):
        dx, dy = SIDES[side]
        return (gx + dx, gy_ + dy)

    own_copy = pltpu.make_async_copy(psfs, own, own_sem)
    own_copy.start()
    chunk = INNER // 4
    image_copies = []
    for t in range(4):
        sl = pl.ds(t * chunk, chunk)
        image_copies.append(pltpu.make_async_copy(image.at[:, sl], img.at[:, sl], image_sem.at[t]))
        image_copies[-1].start()

    order = (fx, gz, gzp, fy, fyp, gy, iz, ix, pown, phalo)
    table_copies = []
    for i, (src, dst) in enumerate(zip(table_refs, order)):
        table_copies.append(pltpu.make_async_copy(src, dst, table_sem.at[i]))
        table_copies[-1].start()

    barrier = pltpu.get_barrier_semaphore()
    count = jnp.int32(0)
    for side in range(8):
        count = count + present(side).astype(jnp.int32)

        @pl.when(present(side))
        def _():
            pl.semaphore_signal(barrier, inc=1, device_id=place(side), device_id_type=MESH)

    own_copy.wait()

    def node(r, c):
        row = (r * 2 + c) * NODE
        return own[row:row + NODE, :].astype(F32)

    def put(row, value):
        part[row:row + NODE, :] = value.astype(BF16)

    w0, w1 = BLEND[0], BLEND[1]
    for col, at in ((0, 0), (1, 64)):
        n0, n1, n2, n3 = (node(r, col) for r in range(4))
        put(at, (w0 * w1) * (n0 + n1) + (w0 * w0) * n2)
        put(at + NODE, (w0 * w0) * n1 + (w0 * w1) * (n2 + n3))
    put(128, (w0 * w1) * (node(0, 0) + node(0, 1)))
    put(160, (w0 * w1) * (node(3, 0) + node(3, 1)))
    corner = {UL: 0, UR: 1, DL: 6, DR: 7}

    def psf_copy(side, target=None):
        if side in corner:
            src = own.at[pl.ds(corner[side] * NODE, NODE), :]
        else:
            src = part.at[pl.ds(*HALO[side]), :]
        return pltpu.make_async_remote_copy(
            src_ref=src, dst_ref=halo.at[pl.ds(*HALO[BACK[side]]), :],
            send_sem=psend_sem.at[side], recv_sem=precv_sem.at[BACK[side]],
            device_id=place(side if target is None else target), device_id_type=MESH)

    pl.semaphore_wait(barrier, count)
    for side in range(8):
        @pl.when(present(side))
        def _():
            psf_copy(side).start()

        @pl.when(jnp.logical_not(present(side)))
        def _():
            halo[pl.ds(*HALO[side]), :] = jnp.zeros((HALO[side][1], PSFW * PSFW), BF16)

    for copy in table_copies:
        copy.wait()
    width = 512
    for t in range(INNER // width):
        if t % (chunk // width) == 0:
            image_copies[t // (chunk // width)].wait()
        sl = slice(t * width, (t + 1) * width)
        d1[:, sl] = mm(fx[...], img[:, sl].astype(BF16)).astype(BF16)

    def depth_step(ref, table, t, ylo, width_y, stride, out):
        def rhs(tile):
            sl = pl.ds(pl.multiple_of(tile * LANES, LANES), LANES)
            return jnp.concatenate([ref[:LANES, sl], ref[LANES:, sl]], axis=1)

        both = jnp.concatenate([rhs(2 * t), rhs(2 * t + 1)], axis=0)
        res = mm_t(table[...], both)
        for jj in range(2):
            for part in range(2):
                for y in range(ylo):
                    row = (part * ylo + y) * LZ
                    block = res[row:row + LZ, jj * LANES:(jj + 1) * LANES]
                    start = part * width_y + (2 * t + jj) * ylo + y
                    out[pl.ds(start, LZ, stride=stride), :] = block

    @pl.loop(0, 16, unroll=U_DEPTH)
    def _(t):
        depth_step(d1, gz, t, 2, PATCH, SY, spec)

    def slab(ref, t, rows, stride):
        parts = [ref[pl.ds((2 * t + h) * stride, rows), :] for h in range(2)]
        return jnp.concatenate(parts, axis=1).astype(BF16)

    @pl.loop(0, LZ // 2, unroll=U_IMAGE)
    def _(t):
        ispec[t] = mm(fy[...], slab(spec, t, 2 * PATCH, SY)).astype(BF16)

    for side in range(8):
        @pl.when(present(side))
        def _():
            psf_copy(BACK[side], side).wait_recv()
    for t in range(2):
        sl = slice(t * 512, (t + 1) * 512)
        e1[:, sl] = (mm(pown[...], own[:, sl]) + mm(phalo[...], halo[:, sl])).astype(BF16)

    @pl.loop(0, 4, unroll=U_PSF)
    def _(t):
        depth_step(e1, gzp, t, 4, PSFW, SP, pspec)

    @pl.loop(0, LZ // 2, unroll=U_BACK)
    def _(t):
        b = mm(fyp[...], slab(pspec, t, 2 * PSFW, SP)).astype(BF16)
        a = ispec[t]
        ar, ai, br, bi = a[:LXY], a[LXY:], b[:LXY], b[LXY:]
        prod = jnp.concatenate([ar * br - ai * bi, ar * bi + ai * br], axis=0)
        back = mm(gy[...], prod)
        for h in range(2):
            for part_ in range(2):
                block = back[part_ * LXY:(part_ + 1) * LXY, h * LANES:(h + 1) * LANES]
                resp[pl.ds(part_ * LZ + 2 * t + h, LXY, stride=SZ), :] = block

    def group(g):
        rows = []
        for h in range(2):
            parts = [resp[pl.ds((4 * g + 2 * h + q) * SZ, 2 * LZ), :] for q in range(2)]
            flat = jnp.concatenate(parts, axis=1).astype(BF16)
            z = mm(iz[...], flat).astype(BF16)
            for q in range(2):
                half = z[:, q * LANES:(q + 1) * LANES]
                rows.append(jnp.concatenate([half[:DEPTH], half[DEPTH:]], axis=1))
        return mm_t(ix[...], jnp.concatenate(rows, axis=0))

    for side in range(2):
        @pl.loop(0, EDGE, unroll=EDGE)
        def _(e):
            cols = pl.ds(pl.multiple_of(e * 256, 256), 256)
            ysend[side, :, cols] = group(e + side * (GROUPS - EDGE)).astype(BF16)

    def y_copy(side, target):
        dx, dy = SIDES[side]
        rows = {0: pl.ds(HALF, TILE), -1: pl.ds(0, HALF), 1: pl.ds(HALF + TILE, HALF)}[dx]
        dst = yrecv.at[BACK[side]] if dx == 0 else crecv.at[BACK[side] - 4]
        return pltpu.make_async_remote_copy(
            src_ref=ysend.at[side if dx == 0 else (dy + 1) // 2, rows, :], dst_ref=dst,
            send_sem=rsend_sem.at[side], recv_sem=rrecv_sem.at[BACK[side]],
            device_id=place(side if target is None else target), device_id_type=MESH)

    def x_copy(side, target):
        return pltpu.make_async_remote_copy(
            src_ref=xsend.at[side - 2], dst_ref=xrecv.at[BACK[side] - 2],
            send_sem=rsend_sem.at[side], recv_sem=rrecv_sem.at[BACK[side]],
            device_id=place(side if target is None else target), device_id_type=MESH)

    def response_copy(side, target=None):
        return (x_copy if side in (UP, DOWN) else y_copy)(side, target)

    for side in (LEFT, RIGHT, UL, UR, DL, DR):
        @pl.when(present(side))
        def _():
            response_copy(side).start()

    @pl.loop(0, GROUPS - 2 * EDGE, unroll=U_INNER)
    def _(g):
        cols = pl.ds(pl.multiple_of(g * 256, 256), 256)
        value = group(g + EDGE)
        out[:, cols] = value[HALF:HALF + TILE]
        xsend[0, :, cols] = value[:HALF].astype(BF16)
        xsend[1, :, cols] = value[HALF + TILE:].astype(BF16)

    for side in (UP, DOWN):
        @pl.when(present(side))
        def _():
            response_copy(side).start()

    def arrive(side, rows, cols, ref):
        @pl.when(present(side))
        def _():
            response_copy(BACK[side], side).wait_recv()
            out[rows, cols] += ref[...].astype(F32)

    top, bottom = pl.ds(0, HALF), pl.ds(TILE - HALF, HALF)
    first, last = pl.ds(0, BAND), pl.ds(INNER - BAND, BAND)
    every = pl.ds(0, TILE)
    arrive(UP, top, pl.ds(0, INNER), xrecv.at[0])
    arrive(DOWN, bottom, pl.ds(0, INNER), xrecv.at[1])
    arrive(UL, top, first, crecv.at[0])
    arrive(DL, bottom, first, crecv.at[2])
    arrive(LEFT, every, first, yrecv.at[0])
    arrive(UR, top, last, crecv.at[1])
    arrive(DR, bottom, last, crecv.at[3])
    arrive(RIGHT, every, last, yrecv.at[1])
    for side in range(8):
        @pl.when(present(side))
        def _():
            psf_copy(side).wait_send()
            response_copy(side).wait_send()


def compute(image, psfs, *consts):
    vmem, anywhere = pl.BlockSpec(memory_space=pltpu.VMEM), pl.BlockSpec(memory_space=pltpu.HBM)
    dma = pltpu.SemaphoreType.DMA
    return pl.pallas_call(
        kernel,
        out_shape=jax.ShapeDtypeStruct((TILE, INNER), F32),
        in_specs=[anywhere] * (2 + len(consts)),
        out_specs=vmem,
        scratch_shapes=[
            pltpu.VMEM((TILE, INNER), F32),
            pltpu.VMEM((8 * PSFW, PSFW * PSFW), BF16),
            pltpu.VMEM((6 * PSFW, PSFW * PSFW), BF16),
            pltpu.VMEM((10 * PSFW, PSFW * PSFW), BF16),
            pltpu.VMEM((2 * LANES, INNER), BF16),
            pltpu.VMEM((2 * LANES, PSFW * PSFW), BF16),
            pltpu.VMEM((LZ * SY, LANES), F32),
            pltpu.VMEM((LZ * SP, LANES), F32),
            pltpu.VMEM((LZ // 2, 2 * LXY, 2 * LANES), BF16),
            pltpu.VMEM((LXY * SZ, LANES), F32),
            pltpu.VMEM((2, EXT, BAND), BF16),
            pltpu.VMEM((2, HALF, INNER), BF16),
            pltpu.VMEM((2, TILE, BAND), BF16),
            pltpu.VMEM((2, HALF, INNER), BF16),
            pltpu.VMEM((4, HALF, BAND), BF16),
            *[pltpu.VMEM(c.shape, BF16) for c in consts],
            dma((4,)), dma, dma((len(consts),)), dma((8,)), dma((8,)), dma((8,)), dma((8,)),
        ],
        compiler_params=pltpu.CompilerParams(
            vmem_limit_bytes=40 * 1024 * 1024, collective_id=0, has_side_effects=True),
    )(*[pltpu.with_memory_space_constraint(v, pltpu.HBM) for v in (image, psfs.reshape(8 * PSFW, PSFW * PSFW), *consts)])


def body(image, psfs):
    return compute(image, psfs, *tables())


def solution(mesh):
    placed = (P("gx", "gy"), P("gx", "gy", None, None))
    return jax.shard_map(body, mesh=mesh, in_specs=placed, out_specs=P("gx", "gy"), check_vma=False)
```

```python
import math

import jax
import jax.numpy as jnp
import numpy as np
from jax import lax
from jax.experimental import pallas as pl
from jax.experimental.pallas import tpu as pltpu
from jax.sharding import PartitionSpec as P

PATCH = 64
PSFW = 32
DEPTH = 64
HALF = PSFW // 2
LXY = PATCH + PSFW
LZ = DEPTH + HALF
BINS = LXY // 2
PATCHES = 2
LANES = 128
TILE = PATCHES * PATCH
EXT = TILE + PSFW
SY = 2 * PATCH + 4
SP = 2 * PSFW + 4
SZ = 2 * LZ + 4
COLS = LXY * DEPTH
BLEND = (0.125, 0.375, 0.375, 0.125)
CORNER = BLEND[0] * BLEND[0]
PIECES = ((0, 1), (1, 1), (0, 1), (1, 1), (0, 1), (1, 1), (0, CORNER), (0, CORNER), (1, CORNER), (1, CORNER))
BAND = HALF * DEPTH
INNER = PATCH * DEPTH
MESH = pl.DeviceIdType.MESH
F32 = jnp.float32
BF16 = jnp.bfloat16


def tables():
    theta = 2.0 * math.pi * (np.arange(BINS) + 0.5) / LXY

    fx = np.zeros((2, LANES, PATCHES, PATCH))
    ang = theta[:, None] * np.arange(PATCH)[None, :]
    for p in range(PATCHES):
        fx[0, p * BINS:(p + 1) * BINS, p] = np.cos(ang)
        fx[1, p * BINS:(p + 1) * BINS, p] = -np.sin(ang)
    fx = fx.reshape(2 * LANES, TILE)

    ang = theta[:, None] * np.arange(PSFW)[None, :]
    bare = np.stack([np.cos(ang), -np.sin(ang)])
    own = np.zeros((2, LANES, 2 * PATCHES, 2, PSFW))
    for p in range(PATCHES):
        for a in range(4):
            row = 2 * p + a - 1
            if 0 <= row < 2 * PATCHES:
                for col in range(2):
                    own[:, p * BINS:(p + 1) * BINS, row, col] = BLEND[a] * BLEND[col + 1] * bare
    own = own.reshape(2 * LANES, -1)
    halo = np.zeros((2, LANES, len(PIECES), PSFW))
    for i, (p, weight) in enumerate(PIECES):
        halo[:, p * BINS:(p + 1) * BINS, i] = weight * bare
    halo = halo.reshape(2 * LANES, -1)

    def pair(cos, sin, sign):
        return np.stack([np.stack([cos, -sign * sin]), np.stack([sign * sin, cos])])

    def depth(count, depths):
        ang = 2.0 * math.pi / LZ * np.outer(np.arange(LZ), np.arange(depths))
        quad = pair(np.cos(ang), np.sin(ang), -1.0)
        out = np.zeros((2, count, LZ, 2, count, depths))
        for y in range(count):
            out[:, y, :, :, y, :] = quad.transpose(0, 2, 1, 3)
        return out.reshape(2 * count * LZ, 2 * count * depths)

    gz = depth(2, DEPTH)
    gzp = depth(4, PSFW)

    def flat(quad):
        o, i, r, c = quad.shape
        return quad.transpose(0, 2, 1, 3).reshape(o * r, i * c)

    ang = 2.0 * math.pi / LXY * np.outer(np.arange(LXY), np.arange(LXY))
    full = pair(np.cos(ang), np.sin(ang), -1.0)
    fy = flat(full[:, :, :, :PATCH])
    fyp = flat(full[:, :, :, :PSFW])
    gy = flat(pair(np.cos(ang), np.sin(ang), 1.0)) / LXY

    ang = 2.0 * math.pi / LZ * np.outer(np.arange(DEPTH) + HALF, np.arange(LZ))
    iz = flat(pair(np.cos(ang), np.sin(ang), 1.0)) / LZ

    ix = np.zeros((EXT, 2, LANES))
    ang = np.arange(LXY)[:, None] * theta[None, :]
    for p in range(PATCHES):
        ix[p * PATCH:p * PATCH + LXY, 0, p * BINS:(p + 1) * BINS] = np.cos(ang) * 2.0 / LXY
        ix[p * PATCH:p * PATCH + LXY, 1, p * BINS:(p + 1) * BINS] = -np.sin(ang) * 2.0 / LXY
    ix = ix.reshape(EXT, 2 * LANES)

    return [jnp.asarray(t, BF16) for t in [fx, gz, gzp, fy, fyp, gy, iz, ix, own, halo]]


def mm(a, b):
    return lax.dot_general(a, b, (((1,), (0,)), ((), ())), preferred_element_type=F32)


def mm_t(a, b):
    return lax.dot_general(a, b, (((1,), (1,)), ((), ())), preferred_element_type=F32)


SIDES = ((0, -1), (0, 1), (-1, 0), (1, 0), (-1, -1), (-1, 1), (1, -1), (1, 1))
LEFT, RIGHT, UP, DOWN, UL, UR, DL, DR = range(8)
BACK = (RIGHT, LEFT, DOWN, UP, DR, DL, UR, UL)
HALO = ((0, 64), (64, 64), (128, 32), (160, 32), (192, 32), (224, 32), (256, 32), (288, 32))
NODE = PSFW
GROUPS = LXY // 4
U_DEPTH, U_IMAGE, U_PSF, U_BACK, U_INNER = 16, 40, 4, 40, 16
EDGE = HALF // 4


def kernel(image, psfs, *refs):
    kernel_body(image, psfs, refs[:10], *refs[10:])


def kernel_body(image, psfs, table_refs,
           out,
           img, own, part, halo, d1, e1, spec, pspec, ispec, resp,
           ysend, xsend, esend, yrecv, xrecv, erecv, crecv,
           fx, gz, gzp, fy, fyp, gy, iz, ix, pown, phalo,
           image_sem, own_sem, table_sem, psend_sem, precv_sem, rsend_sem, rrecv_sem):
    gx, gy_ = lax.axis_index("gx"), lax.axis_index("gy")
    last_x, last_y = lax.axis_size("gx") - 1, lax.axis_size("gy") - 1

    def present(side):
        dx, dy = SIDES[side]
        terms = []
        if dx:
            terms.append(gx > 0 if dx < 0 else gx < last_x)
        if dy:
            terms.append(gy_ > 0 if dy < 0 else gy_ < last_y)
        return terms[0] if len(terms) == 1 else jnp.logical_and(terms[0], terms[1])

    def place(side):
        dx, dy = SIDES[side]
        return (gx + dx, gy_ + dy)

    own_copy = pltpu.make_async_copy(psfs, own, own_sem)
    own_copy.start()
    order = (fx, gz, gzp, fy, fyp, gy, iz, ix, pown, phalo)
    tables_in = {}
    for i, (src, dst) in enumerate(zip(table_refs, order)):
        tables_in[i] = pltpu.make_async_copy(src, dst, table_sem.at[i])
    chunk = INNER // 4
    image_copies = []
    for t in range(4):
        sl = pl.ds(t * chunk, chunk)
        image_copies.append(pltpu.make_async_copy(image.at[:, sl], img.at[:, sl], image_sem.at[t]))
    tables_in[0].start()
    for copy in image_copies:
        copy.start()
    for i in range(1, len(order)):
        tables_in[i].start()

    barrier = pltpu.get_barrier_semaphore()
    count = jnp.int32(0)
    for side in range(8):
        count = count + present(side).astype(jnp.int32)

        @pl.when(present(side))
        def _():
            pl.semaphore_signal(barrier, inc=1, device_id=place(side), device_id_type=MESH)

    own_copy.wait()
    corner = {UL: 0, UR: 1, DL: 6, DR: 7}

    def psf_copy(side, target=None):
        if side in corner:
            src = own.at[pl.ds(corner[side] * NODE, NODE), :]
        else:
            src = part.at[pl.ds(*HALO[side]), :]
        return pltpu.make_async_remote_copy(
            src_ref=src, dst_ref=halo.at[pl.ds(*HALO[BACK[side]]), :],
            send_sem=psend_sem.at[side], recv_sem=precv_sem.at[BACK[side]],
            device_id=place(side if target is None else target), device_id_type=MESH)

    pl.semaphore_wait(barrier, count)
    for side in range(4, 8):
        @pl.when(present(side))
        def _():
            psf_copy(side).start()

    def node(r, c):
        row = (r * 2 + c) * NODE
        return own[row:row + NODE, :].astype(F32)

    def put(row, value):
        part[row:row + NODE, :] = value.astype(BF16)

    w0, w1 = BLEND[0], BLEND[1]
    for col, at in ((0, 0), (1, 64)):
        n0, n1, n2, n3 = (node(r, col) for r in range(4))
        put(at, (w0 * w1) * (n0 + n1) + (w0 * w0) * n2)
        put(at + NODE, (w0 * w0) * n1 + (w0 * w1) * (n2 + n3))
    put(128, (w0 * w1) * (node(0, 0) + node(0, 1)))
    put(160, (w0 * w1) * (node(3, 0) + node(3, 1)))
    for side in range(8):
        if side < 4:
            @pl.when(present(side))
            def _():
                psf_copy(side).start()

        @pl.when(jnp.logical_not(present(side)))
        def _():
            halo[pl.ds(*HALO[side]), :] = jnp.zeros((HALO[side][1], PSFW * PSFW), BF16)

    tables_in[0].wait()
    width = 512
    for t in range(INNER // width):
        if t % (chunk // width) == 0:
            image_copies[t // (chunk // width)].wait()
        sl = slice(t * width, (t + 1) * width)
        d1[:, sl] = mm(fx[...], img[:, sl].astype(BF16)).astype(BF16)

    def depth_step(ref, table, t, ylo, width_y, stride, out):
        def rhs(tile):
            sl = pl.ds(pl.multiple_of(tile * LANES, LANES), LANES)
            return jnp.concatenate([ref[:LANES, sl], ref[LANES:, sl]], axis=1)

        both = jnp.concatenate([rhs(2 * t), rhs(2 * t + 1)], axis=0)
        res = mm_t(table[...], both)
        for jj in range(2):
            for part in range(2):
                for y in range(ylo):
                    row = (part * ylo + y) * LZ
                    block = res[row:row + LZ, jj * LANES:(jj + 1) * LANES]
                    start = part * width_y + (2 * t + jj) * ylo + y
                    out[pl.ds(start, LZ, stride=stride), :] = block

    for i in range(1, len(order)):
        tables_in[i].wait()

    @pl.loop(0, 16, unroll=U_DEPTH)
    def _(t):
        depth_step(d1, gz, t, 2, PATCH, SY, spec)

    def slab(ref, t, rows, stride):
        parts = [ref[pl.ds((2 * t + h) * stride, rows), :] for h in range(2)]
        return jnp.concatenate(parts, axis=1).astype(BF16)

    @pl.loop(0, LZ // 2, unroll=U_IMAGE)
    def _(t):
        ispec[t] = mm(fy[...], slab(spec, t, 2 * PATCH, SY)).astype(BF16)

    for side in range(8):
        @pl.when(present(side))
        def _():
            psf_copy(BACK[side], side).wait_recv()
    for t in range(2):
        sl = slice(t * 512, (t + 1) * 512)
        e1[:, sl] = (mm(pown[...], own[:, sl]) + mm(phalo[...], halo[:, sl])).astype(BF16)

    @pl.loop(0, 4, unroll=U_PSF)
    def _(t):
        depth_step(e1, gzp, t, 4, PSFW, SP, pspec)

    @pl.loop(0, LZ // 2, unroll=U_BACK)
    def _(t):
        b = mm(fyp[...], slab(pspec, t, 2 * PSFW, SP)).astype(BF16)
        a = ispec[t]
        ar, ai, br, bi = a[:LXY], a[LXY:], b[:LXY], b[LXY:]
        prod = jnp.concatenate([ar * br - ai * bi, ar * bi + ai * br], axis=0)
        back = mm(gy[...], prod)
        for h in range(2):
            for part_ in range(2):
                block = back[part_ * LXY:(part_ + 1) * LXY, h * LANES:(h + 1) * LANES]
                resp[pl.ds(part_ * LZ + 2 * t + h, LXY, stride=SZ), :] = block

    def group(g):
        rows = []
        for h in range(2):
            parts = [resp[pl.ds((4 * g + 2 * h + q) * SZ, 2 * LZ), :] for q in range(2)]
            flat = jnp.concatenate(parts, axis=1).astype(BF16)
            z = mm(iz[...], flat).astype(BF16)
            for q in range(2):
                half = z[:, q * LANES:(q + 1) * LANES]
                rows.append(jnp.concatenate([half[:DEPTH], half[DEPTH:]], axis=1))
        return mm_t(ix[...], jnp.concatenate(rows, axis=0))

    for side in range(2):
        @pl.loop(0, EDGE, unroll=EDGE)
        def _(e):
            cols = pl.ds(pl.multiple_of(e * 256, 256), 256)
            ysend[side, :, cols] = group(e + side * (GROUPS - EDGE)).astype(BF16)

    def remote(src, dst, send_sem, recv_sem, at, side, target):
        return pltpu.make_async_remote_copy(
            src_ref=src, dst_ref=dst, send_sem=send_sem.at[at + side], recv_sem=recv_sem.at[at + BACK[side]],
            device_id=place(side if target is None else target), device_id_type=MESH)

    mid = TILE - 2 * HALF
    inner = pl.ds(2 * HALF, mid)

    def mid_copy(side, target=None):
        return remote(ysend.at[side, inner, :], yrecv.at[BACK[side]], rsend_sem, rrecv_sem, 0, side, target)

    def corner_copy(side, target=None):
        rows = pl.ds(0 if side == UP else HALF + TILE, HALF)
        return remote(ysend.at[:, rows, :], crecv.at[BACK[side] - 2], rsend_sem, rrecv_sem, 0, side, target)

    def edge_copy(side, target=None):
        return remote(esend.at[side], erecv.at[BACK[side]], rsend_sem, rrecv_sem, 4, side, target)

    def band_copy(side, target=None):
        return remote(xsend.at[side - 2], xrecv.at[BACK[side] - 2], rsend_sem, rrecv_sem, 4, side, target)

    first_copy = (mid_copy, mid_copy, corner_copy, corner_copy)
    second_copy = (edge_copy, edge_copy, band_copy, band_copy)

    for side in (UP, DOWN, LEFT, RIGHT):
        @pl.when(present(side))
        def _():
            first_copy[side](side).start()

    for side in (UP, DOWN):
        @pl.when(jnp.logical_not(present(side)))
        def _():
            crecv[side - 2] = jnp.zeros((2, HALF, BAND), BF16)

    @pl.loop(0, GROUPS - 2 * EDGE, unroll=U_INNER)
    def _(g):
        cols = pl.ds(pl.multiple_of(g * 256, 256), 256)
        value = group(g + EDGE)
        out[:, cols] = value[HALF:HALF + TILE]
        xsend[0, :, cols] = value[:HALF].astype(BF16)
        xsend[1, :, cols] = value[HALF + TILE:].astype(BF16)

    for side in (UP, DOWN):
        @pl.when(present(side))
        def _():
            band_copy(side).start()

    for side in (UP, DOWN):
        @pl.when(present(side))
        def _():
            corner_copy(BACK[side], side).wait_recv()

    for side in (LEFT, RIGHT):
        for end in range(2):
            rows = slice(HALF + end * (TILE - HALF), 2 * HALF + end * (TILE - HALF))
            esend[side, end] = (ysend[side, rows, :].astype(F32) + crecv[end, side].astype(F32)).astype(BF16)

        @pl.when(present(side))
        def _():
            edge_copy(side).start()

    top, bottom = pl.ds(0, HALF), pl.ds(TILE - HALF, HALF)
    columns = (pl.ds(0, BAND), pl.ds(INNER - BAND, BAND))
    for side, rows in ((UP, top), (DOWN, bottom)):
        @pl.when(present(side))
        def _():
            band_copy(BACK[side], side).wait_recv()
            out[rows, :] += xrecv[side - 2].astype(F32)

    for side in (LEFT, RIGHT):
        @pl.when(present(side))
        def _():
            mid_copy(BACK[side], side).wait_recv()
            out[pl.ds(HALF, mid), columns[side]] += yrecv[side].astype(F32)
            edge_copy(BACK[side], side).wait_recv()
            out[top, columns[side]] += erecv[side, 0].astype(F32)
            out[bottom, columns[side]] += erecv[side, 1].astype(F32)

    for side in range(8):
        @pl.when(present(side))
        def _():
            psf_copy(side).wait_send()

    for side in range(4):
        @pl.when(present(side))
        def _():
            first_copy[side](side).wait_send()
            second_copy[side](side).wait_send()


def compute(image, psfs, *consts):
    vmem, anywhere = pl.BlockSpec(memory_space=pltpu.VMEM), pl.BlockSpec(memory_space=pltpu.HBM)
    dma = pltpu.SemaphoreType.DMA
    return pl.pallas_call(
        kernel,
        out_shape=jax.ShapeDtypeStruct((TILE, INNER), F32),
        in_specs=[anywhere] * (2 + len(consts)),
        out_specs=vmem,
        scratch_shapes=[
            pltpu.VMEM((TILE, INNER), F32),
            pltpu.VMEM((8 * PSFW, PSFW * PSFW), BF16),
            pltpu.VMEM((6 * PSFW, PSFW * PSFW), BF16),
            pltpu.VMEM((10 * PSFW, PSFW * PSFW), BF16),
            pltpu.VMEM((2 * LANES, INNER), BF16),
            pltpu.VMEM((2 * LANES, PSFW * PSFW), BF16),
            pltpu.VMEM((LZ * SY, LANES), F32),
            pltpu.VMEM((LZ * SP, LANES), F32),
            pltpu.VMEM((LZ // 2, 2 * LXY, 2 * LANES), BF16),
            pltpu.VMEM((LXY * SZ, LANES), F32),
            pltpu.VMEM((2, EXT, BAND), BF16),
            pltpu.VMEM((2, HALF, INNER), BF16),
            pltpu.VMEM((2, 2, HALF, BAND), BF16),
            pltpu.VMEM((2, TILE - 2 * HALF, BAND), BF16),
            pltpu.VMEM((2, HALF, INNER), BF16),
            pltpu.VMEM((2, 2, HALF, BAND), BF16),
            pltpu.VMEM((2, 2, HALF, BAND), BF16),
            *[pltpu.VMEM(c.shape, BF16) for c in consts],
            dma((4,)), dma, dma((len(consts),)), dma((8,)), dma((8,)), dma((8,)), dma((8,)),
        ],
        compiler_params=pltpu.CompilerParams(
            vmem_limit_bytes=40 * 1024 * 1024, collective_id=0, has_side_effects=True),
    )(*[pltpu.with_memory_space_constraint(v, pltpu.HBM) for v in (image, psfs.reshape(8 * PSFW, PSFW * PSFW), *consts)])


def body(image, psfs):
    return compute(image, psfs, *tables())


def solution(mesh):
    placed = (P("gx", "gy"), P("gx", "gy", None, None))
    return jax.shard_map(body, mesh=mesh, in_specs=placed, out_specs=P("gx", "gy"), check_vma=False)
```

```python
import math

import jax
import jax.numpy as jnp
import numpy as np
from jax import lax
from jax.experimental import pallas as pl
from jax.experimental.pallas import tpu as pltpu
from jax.sharding import PartitionSpec as P

PATCH = 64
PSFW = 32
DEPTH = 64
HALF = PSFW // 2
LXY = PATCH + PSFW
LZ = DEPTH + HALF
BINS = LXY // 2
PATCHES = 2
LANES = 128
TILE = PATCHES * PATCH
EXT = TILE + PSFW
SY = 2 * PATCH + 4
SP = 2 * PSFW + 4
SZ = 2 * LZ + 4
COLS = LXY * DEPTH
BLEND = (0.125, 0.375, 0.375, 0.125)
CORNER = BLEND[0] * BLEND[0]
PIECES = ((0, 1), (1, 1), (0, 1), (1, 1), (0, 1), (1, 1), (0, CORNER), (0, CORNER), (1, CORNER), (1, CORNER))
BAND = HALF * DEPTH
INNER = PATCH * DEPTH
MESH = pl.DeviceIdType.MESH
F32 = jnp.float32
BF16 = jnp.bfloat16


def tables():
    theta = 2.0 * math.pi * (np.arange(BINS) + 0.5) / LXY

    fx = np.zeros((2, LANES, PATCHES, PATCH))
    ang = theta[:, None] * np.arange(PATCH)[None, :]
    for p in range(PATCHES):
        fx[0, p * BINS:(p + 1) * BINS, p] = np.cos(ang)
        fx[1, p * BINS:(p + 1) * BINS, p] = -np.sin(ang)
    fx = fx.reshape(2 * LANES, TILE)

    ang = theta[:, None] * np.arange(PSFW)[None, :]
    bare = np.stack([np.cos(ang), -np.sin(ang)])
    own = np.zeros((2, LANES, 2 * PATCHES, 2, PSFW))
    for p in range(PATCHES):
        for a in range(4):
            row = 2 * p + a - 1
            if 0 <= row < 2 * PATCHES:
                for col in range(2):
                    own[:, p * BINS:(p + 1) * BINS, row, col] = BLEND[a] * BLEND[col + 1] * bare
    own = own.reshape(2 * LANES, -1)
    halo = np.zeros((2, LANES, len(PIECES), PSFW))
    for i, (p, weight) in enumerate(PIECES):
        halo[:, p * BINS:(p + 1) * BINS, i] = weight * bare
    halo = halo.reshape(2 * LANES, -1)

    def pair(cos, sin, sign):
        return np.stack([np.stack([cos, -sign * sin]), np.stack([sign * sin, cos])])

    def depth(count, depths):
        ang = 2.0 * math.pi / LZ * np.outer(np.arange(LZ), np.arange(depths))
        quad = pair(np.cos(ang), np.sin(ang), -1.0)
        out = np.zeros((2, count, LZ, 2, count, depths))
        for y in range(count):
            out[:, y, :, :, y, :] = quad.transpose(0, 2, 1, 3)
        return out.reshape(2 * count * LZ, 2 * count * depths)

    gz = depth(2, DEPTH)
    gzp = depth(4, PSFW)

    def flat(quad):
        o, i, r, c = quad.shape
        return quad.transpose(0, 2, 1, 3).reshape(o * r, i * c)

    ang = 2.0 * math.pi / LXY * np.outer(np.arange(LXY), np.arange(LXY))
    full = pair(np.cos(ang), np.sin(ang), -1.0)
    fy = flat(full[:, :, :, :PATCH])
    fyp = flat(full[:, :, :, :PSFW])
    gy = flat(pair(np.cos(ang), np.sin(ang), 1.0)) / LXY

    ang = 2.0 * math.pi / LZ * np.outer(np.arange(DEPTH) + HALF, np.arange(LZ))
    iz = flat(pair(np.cos(ang), np.sin(ang), 1.0)) / LZ

    ix = np.zeros((EXT, 2, LANES))
    ang = np.arange(LXY)[:, None] * theta[None, :]
    for p in range(PATCHES):
        ix[p * PATCH:p * PATCH + LXY, 0, p * BINS:(p + 1) * BINS] = np.cos(ang) * 2.0 / LXY
        ix[p * PATCH:p * PATCH + LXY, 1, p * BINS:(p + 1) * BINS] = -np.sin(ang) * 2.0 / LXY
    ix = ix.reshape(EXT, 2 * LANES)

    return [jnp.asarray(t, BF16) for t in [fx, gz, gzp, fy, fyp, gy, iz, ix, own, halo]]


def mm(a, b):
    return lax.dot_general(a, b, (((1,), (0,)), ((), ())), preferred_element_type=F32)


def mm_t(a, b):
    return lax.dot_general(a, b, (((1,), (1,)), ((), ())), preferred_element_type=F32)


SIDES = ((0, -1), (0, 1), (-1, 0), (1, 0), (-1, -1), (-1, 1), (1, -1), (1, 1))
LEFT, RIGHT, UP, DOWN, UL, UR, DL, DR = range(8)
BACK = (RIGHT, LEFT, DOWN, UP, DR, DL, UR, UL)
HALO = ((0, 64), (64, 64), (128, 32), (160, 32), (192, 32), (224, 32), (256, 32), (288, 32))
NODE = PSFW
GROUPS = LXY // 4
U_DEPTH, U_IMAGE, U_PSF, U_BACK, U_INNER = 16, 40, 4, 40, 16
EDGE = HALF // 4


def kernel(image, psfs, *refs):
    kernel_body(image, psfs, refs[:10], *refs[10:])


def kernel_body(image, psfs, table_refs,
           out,
           img, own, part, halo, d1, e1, spec, pspec, ispec, resp,
           ysend, xsend, esend, yrecv, xrecv, erecv, crecv,
           fx, gz, gzp, fy, fyp, gy, iz, ix, pown, phalo,
           image_sem, own_sem, table_sem, psend_sem, precv_sem, rsend_sem, rrecv_sem):
    gx, gy_ = lax.axis_index("gx"), lax.axis_index("gy")
    last_x, last_y = lax.axis_size("gx") - 1, lax.axis_size("gy") - 1

    def present(side):
        dx, dy = SIDES[side]
        terms = []
        if dx:
            terms.append(gx > 0 if dx < 0 else gx < last_x)
        if dy:
            terms.append(gy_ > 0 if dy < 0 else gy_ < last_y)
        return terms[0] if len(terms) == 1 else jnp.logical_and(terms[0], terms[1])

    def place(side):
        dx, dy = SIDES[side]
        return (gx + dx, gy_ + dy)

    own_copy = pltpu.make_async_copy(psfs, own, own_sem)
    own_copy.start()
    order = (fx, gz, gzp, fy, fyp, gy, iz, ix, pown, phalo)
    tables_in = {}
    for i, (src, dst) in enumerate(zip(table_refs, order)):
        tables_in[i] = pltpu.make_async_copy(src, dst, table_sem.at[i])
    chunk = INNER // 4
    image_copies = []
    for t in range(4):
        sl = pl.ds(t * chunk, chunk)
        image_copies.append(pltpu.make_async_copy(image.at[:, sl], img.at[:, sl], image_sem.at[t]))
    tables_in[0].start()
    for copy in image_copies:
        copy.start()
    for i in range(1, len(order)):
        tables_in[i].start()

    barrier = pltpu.get_barrier_semaphore()
    count = jnp.int32(0)
    for side in range(8):
        count = count + present(side).astype(jnp.int32)

        @pl.when(present(side))
        def _():
            pl.semaphore_signal(barrier, inc=1, device_id=place(side), device_id_type=MESH)

    own_copy.wait()
    corner = {UL: 0, UR: 1, DL: 6, DR: 7}

    def psf_copy(side, target=None):
        if side in corner:
            src = own.at[pl.ds(corner[side] * NODE, NODE), :]
        else:
            src = part.at[pl.ds(*HALO[side]), :]
        return pltpu.make_async_remote_copy(
            src_ref=src, dst_ref=halo.at[pl.ds(*HALO[BACK[side]]), :],
            send_sem=psend_sem.at[side], recv_sem=precv_sem.at[BACK[side]],
            device_id=place(side if target is None else target), device_id_type=MESH)

    pl.semaphore_wait(barrier, count)
    for side in range(4, 8):
        @pl.when(present(side))
        def _():
            psf_copy(side).start()

    def node(r, c):
        row = (r * 2 + c) * NODE
        return own[row:row + NODE, :].astype(F32)

    def put(row, value):
        part[row:row + NODE, :] = value.astype(BF16)

    w0, w1 = BLEND[0], BLEND[1]
    for col, at in ((0, 0), (1, 64)):
        n0, n1, n2, n3 = (node(r, col) for r in range(4))
        put(at, (w0 * w1) * (n0 + n1) + (w0 * w0) * n2)
        put(at + NODE, (w0 * w0) * n1 + (w0 * w1) * (n2 + n3))
    put(128, (w0 * w1) * (node(0, 0) + node(0, 1)))
    put(160, (w0 * w1) * (node(3, 0) + node(3, 1)))
    for side in range(8):
        if side < 4:
            @pl.when(present(side))
            def _():
                psf_copy(side).start()

        @pl.when(jnp.logical_not(present(side)))
        def _():
            halo[pl.ds(*HALO[side]), :] = jnp.zeros((HALO[side][1], PSFW * PSFW), BF16)

    tables_in[0].wait()
    width = 512
    for t in range(INNER // width):
        if t % (chunk // width) == 0:
            image_copies[t // (chunk // width)].wait()
        sl = slice(t * width, (t + 1) * width)
        d1[:, sl] = mm(fx[...], img[:, sl].astype(BF16)).astype(BF16)

    def depth_step(ref, table, t, ylo, width_y, stride, out):
        def rhs(tile):
            sl = pl.ds(pl.multiple_of(tile * LANES, LANES), LANES)
            return jnp.concatenate([ref[:LANES, sl], ref[LANES:, sl]], axis=1)

        both = jnp.concatenate([rhs(2 * t), rhs(2 * t + 1)], axis=0)
        res = mm_t(table[...], both)
        for jj in range(2):
            for part in range(2):
                for y in range(ylo):
                    row = (part * ylo + y) * LZ
                    block = res[row:row + LZ, jj * LANES:(jj + 1) * LANES]
                    start = part * width_y + (2 * t + jj) * ylo + y
                    out[pl.ds(start, LZ, stride=stride), :] = block

    for i in range(1, len(order)):
        tables_in[i].wait()

    @pl.loop(0, 16, unroll=U_DEPTH)
    def _(t):
        depth_step(d1, gz, t, 2, PATCH, SY, spec)

    def slab(ref, t, rows, stride):
        parts = [ref[pl.ds((2 * t + h) * stride, rows), :] for h in range(2)]
        return jnp.concatenate(parts, axis=1).astype(BF16)

    @pl.loop(0, LZ // 2, unroll=U_IMAGE)
    def _(t):
        ispec[t] = mm(fy[...], slab(spec, t, 2 * PATCH, SY)).astype(BF16)

    for side in range(8):
        @pl.when(present(side))
        def _():
            psf_copy(BACK[side], side).wait_recv()
    for t in range(2):
        sl = slice(t * 512, (t + 1) * 512)
        e1[:, sl] = (mm(pown[...], own[:, sl]) + mm(phalo[...], halo[:, sl])).astype(BF16)

    @pl.loop(0, 4, unroll=U_PSF)
    def _(t):
        depth_step(e1, gzp, t, 4, PSFW, SP, pspec)

    @pl.loop(0, LZ // 2, unroll=U_BACK)
    def _(t):
        b = mm(fyp[...], slab(pspec, t, 2 * PSFW, SP)).astype(BF16)
        a = ispec[t]
        ar, ai, br, bi = a[:LXY], a[LXY:], b[:LXY], b[LXY:]
        prod = jnp.concatenate([ar * br - ai * bi, ar * bi + ai * br], axis=0)
        back = mm(gy[...], prod)
        for h in range(2):
            for part_ in range(2):
                block = back[part_ * LXY:(part_ + 1) * LXY, h * LANES:(h + 1) * LANES]
                resp[pl.ds(part_ * LZ + 2 * t + h, LXY, stride=SZ), :] = block

    def group(g):
        rows = []
        for h in range(2):
            parts = [resp[pl.ds((4 * g + 2 * h + q) * SZ, 2 * LZ), :] for q in range(2)]
            flat = jnp.concatenate(parts, axis=1).astype(BF16)
            z = mm(iz[...], flat).astype(BF16)
            for q in range(2):
                half = z[:, q * LANES:(q + 1) * LANES]
                rows.append(jnp.concatenate([half[:DEPTH], half[DEPTH:]], axis=1))
        return mm_t(ix[...], jnp.concatenate(rows, axis=0))

    for side in range(2):
        @pl.loop(0, EDGE, unroll=EDGE)
        def _(e):
            cols = pl.ds(pl.multiple_of(e * 256, 256), 256)
            ysend[side, :, cols] = group(e + side * (GROUPS - EDGE)).astype(BF16)

    def remote(src, dst, send_sem, recv_sem, at, side, target):
        return pltpu.make_async_remote_copy(
            src_ref=src, dst_ref=dst, send_sem=send_sem.at[at + side], recv_sem=recv_sem.at[at + BACK[side]],
            device_id=place(side if target is None else target), device_id_type=MESH)

    mid = TILE - 2 * HALF
    inner = pl.ds(2 * HALF, mid)

    def mid_copy(side, target=None):
        return remote(ysend.at[side, inner, :], yrecv.at[BACK[side]], rsend_sem, rrecv_sem, 0, side, target)

    def corner_copy(side, target=None):
        rows = pl.ds(0 if side == UP else HALF + TILE, HALF)
        return remote(ysend.at[:, rows, :], crecv.at[BACK[side] - 2], rsend_sem, rrecv_sem, 0, side, target)

    def edge_copy(side, target=None):
        return remote(esend.at[side], erecv.at[BACK[side]], rsend_sem, rrecv_sem, 4, side, target)

    def band_copy(side, target=None):
        return remote(xsend.at[side - 2], xrecv.at[BACK[side] - 2], rsend_sem, rrecv_sem, 4, side, target)

    first_copy = (mid_copy, mid_copy, corner_copy, corner_copy)
    second_copy = (edge_copy, edge_copy, band_copy, band_copy)

    for side in (UP, DOWN):
        @pl.when(present(side))
        def _():
            first_copy[side](side).start()

    for side in (UP, DOWN):
        @pl.when(jnp.logical_not(present(side)))
        def _():
            crecv[side - 2] = jnp.zeros((2, HALF, BAND), BF16)

    @pl.loop(0, GROUPS - 2 * EDGE, unroll=U_INNER)
    def _(g):
        cols = pl.ds(pl.multiple_of(g * 256, 256), 256)
        value = group(g + EDGE)
        out[:, cols] = value[HALF:HALF + TILE]
        xsend[0, :, cols] = value[:HALF].astype(BF16)
        xsend[1, :, cols] = value[HALF + TILE:].astype(BF16)

    for side in (UP, DOWN):
        @pl.when(present(side))
        def _():
            band_copy(side).start()

    for side in (LEFT, RIGHT):
        @pl.when(present(side))
        def _():
            mid_copy(side).start()

    for side in (UP, DOWN):
        @pl.when(present(side))
        def _():
            corner_copy(BACK[side], side).wait_recv()

    for side in (LEFT, RIGHT):
        for end in range(2):
            rows = slice(HALF + end * (TILE - HALF), 2 * HALF + end * (TILE - HALF))
            esend[side, end] = (ysend[side, rows, :].astype(F32) + crecv[end, side].astype(F32)).astype(BF16)

        @pl.when(present(side))
        def _():
            edge_copy(side).start()

    top, bottom = pl.ds(0, HALF), pl.ds(TILE - HALF, HALF)
    columns = (pl.ds(0, BAND), pl.ds(INNER - BAND, BAND))
    for side, rows in ((UP, top), (DOWN, bottom)):
        @pl.when(present(side))
        def _():
            band_copy(BACK[side], side).wait_recv()
            out[rows, :] += xrecv[side - 2].astype(F32)

    for side in (LEFT, RIGHT):
        @pl.when(present(side))
        def _():
            mid_copy(BACK[side], side).wait_recv()
            out[pl.ds(HALF, mid), columns[side]] += yrecv[side].astype(F32)
            edge_copy(BACK[side], side).wait_recv()
            out[top, columns[side]] += erecv[side, 0].astype(F32)
            out[bottom, columns[side]] += erecv[side, 1].astype(F32)

    for side in range(8):
        @pl.when(present(side))
        def _():
            psf_copy(side).wait_send()

    for side in range(4):
        @pl.when(present(side))
        def _():
            first_copy[side](side).wait_send()
            second_copy[side](side).wait_send()


def compute(image, psfs, *consts):
    vmem, anywhere = pl.BlockSpec(memory_space=pltpu.VMEM), pl.BlockSpec(memory_space=pltpu.HBM)
    dma = pltpu.SemaphoreType.DMA
    return pl.pallas_call(
        kernel,
        out_shape=jax.ShapeDtypeStruct((TILE, INNER), F32),
        in_specs=[anywhere] * (2 + len(consts)),
        out_specs=vmem,
        scratch_shapes=[
            pltpu.VMEM((TILE, INNER), F32),
            pltpu.VMEM((8 * PSFW, PSFW * PSFW), BF16),
            pltpu.VMEM((6 * PSFW, PSFW * PSFW), BF16),
            pltpu.VMEM((10 * PSFW, PSFW * PSFW), BF16),
            pltpu.VMEM((2 * LANES, INNER), BF16),
            pltpu.VMEM((2 * LANES, PSFW * PSFW), BF16),
            pltpu.VMEM((LZ * SY, LANES), F32),
            pltpu.VMEM((LZ * SP, LANES), F32),
            pltpu.VMEM((LZ // 2, 2 * LXY, 2 * LANES), BF16),
            pltpu.VMEM((LXY * SZ, LANES), F32),
            pltpu.VMEM((2, EXT, BAND), BF16),
            pltpu.VMEM((2, HALF, INNER), BF16),
            pltpu.VMEM((2, 2, HALF, BAND), BF16),
            pltpu.VMEM((2, TILE - 2 * HALF, BAND), BF16),
            pltpu.VMEM((2, HALF, INNER), BF16),
            pltpu.VMEM((2, 2, HALF, BAND), BF16),
            pltpu.VMEM((2, 2, HALF, BAND), BF16),
            *[pltpu.VMEM(c.shape, BF16) for c in consts],
            dma((4,)), dma, dma((len(consts),)), dma((8,)), dma((8,)), dma((8,)), dma((8,)),
        ],
        compiler_params=pltpu.CompilerParams(
            vmem_limit_bytes=40 * 1024 * 1024, collective_id=0, has_side_effects=True),
    )(*[pltpu.with_memory_space_constraint(v, pltpu.HBM) for v in (image, psfs.reshape(8 * PSFW, PSFW * PSFW), *consts)])


def body(image, psfs):
    return compute(image, psfs, *tables())


def solution(mesh):
    placed = (P("gx", "gy"), P("gx", "gy", None, None))
    return jax.shard_map(body, mesh=mesh, in_specs=placed, out_specs=P("gx", "gy"), check_vma=False)
```

```python
import math

import jax
import jax.numpy as jnp
import numpy as np
from jax import lax
from jax.experimental import pallas as pl
from jax.experimental.pallas import tpu as pltpu
from jax.sharding import PartitionSpec as P

PATCH = 64
PSFW = 32
DEPTH = 64
HALF = PSFW // 2
LXY = PATCH + PSFW
LZ = DEPTH + HALF
BINS = LXY // 2
PATCHES = 2
LANES = 128
TILE = PATCHES * PATCH
EXT = TILE + PSFW
SY = 2 * PATCH + 4
SP = 2 * PSFW + 4
SZ = 2 * LZ + 4
COLS = LXY * DEPTH
BLEND = (0.125, 0.375, 0.375, 0.125)
CORNER = BLEND[0] * BLEND[0]
PIECES = ((0, 1), (1, 1), (0, 1), (1, 1), (0, 1), (1, 1), (0, CORNER), (0, CORNER), (1, CORNER), (1, CORNER))
BAND = HALF * DEPTH
INNER = PATCH * DEPTH
MESH = pl.DeviceIdType.MESH
F32 = jnp.float32
BF16 = jnp.bfloat16


def tables():
    theta = 2.0 * math.pi * (np.arange(BINS) + 0.5) / LXY

    fx = np.zeros((2, LANES, PATCHES, PATCH))
    ang = theta[:, None] * np.arange(PATCH)[None, :]
    for p in range(PATCHES):
        fx[0, p * BINS:(p + 1) * BINS, p] = np.cos(ang)
        fx[1, p * BINS:(p + 1) * BINS, p] = -np.sin(ang)
    fx = fx.reshape(2 * LANES, TILE)

    ang = theta[:, None] * np.arange(PSFW)[None, :]
    bare = np.stack([np.cos(ang), -np.sin(ang)])
    own = np.zeros((2, LANES, 2 * PATCHES, 2, PSFW))
    for p in range(PATCHES):
        for a in range(4):
            row = 2 * p + a - 1
            if 0 <= row < 2 * PATCHES:
                for col in range(2):
                    own[:, p * BINS:(p + 1) * BINS, row, col] = BLEND[a] * BLEND[col + 1] * bare
    own = own.reshape(2 * LANES, -1)
    halo = np.zeros((2, LANES, len(PIECES), PSFW))
    for i, (p, weight) in enumerate(PIECES):
        halo[:, p * BINS:(p + 1) * BINS, i] = weight * bare
    halo = halo.reshape(2 * LANES, -1)

    def pair(cos, sin, sign):
        return np.stack([np.stack([cos, -sign * sin]), np.stack([sign * sin, cos])])

    def depth(count, depths):
        ang = 2.0 * math.pi / LZ * np.outer(np.arange(LZ), np.arange(depths))
        quad = pair(np.cos(ang), np.sin(ang), -1.0)
        out = np.zeros((2, count, LZ, 2, count, depths))
        for y in range(count):
            out[:, y, :, :, y, :] = quad.transpose(0, 2, 1, 3)
        return out.reshape(2 * count * LZ, 2 * count * depths)

    gz = depth(2, DEPTH)
    gzp = depth(4, PSFW)

    def flat(quad):
        o, i, r, c = quad.shape
        return quad.transpose(0, 2, 1, 3).reshape(o * r, i * c)

    ang = 2.0 * math.pi / LXY * np.outer(np.arange(LXY), np.arange(LXY))
    full = pair(np.cos(ang), np.sin(ang), -1.0)
    fy = flat(full[:, :, :, :PATCH])
    fyp = flat(full[:, :, :, :PSFW])
    gy = flat(pair(np.cos(ang), np.sin(ang), 1.0)) / LXY

    ang = 2.0 * math.pi / LZ * np.outer(np.arange(DEPTH) + HALF, np.arange(LZ))
    iz = flat(pair(np.cos(ang), np.sin(ang), 1.0)) / LZ

    ix = np.zeros((EXT, 2, LANES))
    ang = np.arange(LXY)[:, None] * theta[None, :]
    for p in range(PATCHES):
        ix[p * PATCH:p * PATCH + LXY, 0, p * BINS:(p + 1) * BINS] = np.cos(ang) * 2.0 / LXY
        ix[p * PATCH:p * PATCH + LXY, 1, p * BINS:(p + 1) * BINS] = -np.sin(ang) * 2.0 / LXY
    ix = ix.reshape(EXT, 2 * LANES)

    return [jnp.asarray(t, BF16) for t in [fx, gz, gzp, fy, fyp, gy, iz, ix, own, halo]]


def mm(a, b):
    return lax.dot_general(a, b, (((1,), (0,)), ((), ())), preferred_element_type=F32)


def mm_t(a, b):
    return lax.dot_general(a, b, (((1,), (1,)), ((), ())), preferred_element_type=F32)


SIDES = ((0, -1), (0, 1), (-1, 0), (1, 0), (-1, -1), (-1, 1), (1, -1), (1, 1))
LEFT, RIGHT, UP, DOWN, UL, UR, DL, DR = range(8)
BACK = (RIGHT, LEFT, DOWN, UP, DR, DL, UR, UL)
HALO = ((0, 64), (64, 64), (128, 32), (160, 32), (192, 32), (224, 32), (256, 32), (288, 32))
NODE = PSFW
GROUPS = LXY // 4
U_DEPTH, U_IMAGE, U_PSF, U_BACK, U_INNER = 16, 40, 4, 40, 16
EDGE = HALF // 4


def kernel(image, psfs, *refs):
    kernel_body(image, psfs, refs[:10], *refs[10:])


def kernel_body(image, psfs, table_refs,
           out,
           img, own, part, halo, d1, e1, spec, pspec, ispec, resp,
           ysend, xsend, yrecv, xrecv, crecv,
           fx, gz, gzp, fy, fyp, gy, iz, ix, pown, phalo,
           image_sem, own_sem, table_sem, psend_sem, precv_sem, rsend_sem, rrecv_sem):
    gx, gy_ = lax.axis_index("gx"), lax.axis_index("gy")
    last_x, last_y = lax.axis_size("gx") - 1, lax.axis_size("gy") - 1

    def present(side):
        dx, dy = SIDES[side]
        terms = []
        if dx:
            terms.append(gx > 0 if dx < 0 else gx < last_x)
        if dy:
            terms.append(gy_ > 0 if dy < 0 else gy_ < last_y)
        return terms[0] if len(terms) == 1 else jnp.logical_and(terms[0], terms[1])

    def place(side):
        dx, dy = SIDES[side]
        return (gx + dx, gy_ + dy)

    own_copy = pltpu.make_async_copy(psfs, own, own_sem)
    own_copy.start()
    order = (fx, gz, gzp, fy, fyp, gy, iz, ix, pown, phalo)
    tables_in = {}
    for i, (src, dst) in enumerate(zip(table_refs, order)):
        tables_in[i] = pltpu.make_async_copy(src, dst, table_sem.at[i])
    chunk = INNER // 4
    image_copies = []
    for t in range(4):
        sl = pl.ds(t * chunk, chunk)
        image_copies.append(pltpu.make_async_copy(image.at[:, sl], img.at[:, sl], image_sem.at[t]))
    tables_in[0].start()
    for copy in image_copies:
        copy.start()
    for i in range(1, len(order)):
        tables_in[i].start()

    barrier = pltpu.get_barrier_semaphore()
    count = jnp.int32(0)
    for side in range(8):
        count = count + present(side).astype(jnp.int32)

        @pl.when(present(side))
        def _():
            pl.semaphore_signal(barrier, inc=1, device_id=place(side), device_id_type=MESH)

    own_copy.wait()
    corner = {UL: 0, UR: 1, DL: 6, DR: 7}

    def psf_copy(side, target=None):
        if side in corner:
            src = own.at[pl.ds(corner[side] * NODE, NODE), :]
        else:
            src = part.at[pl.ds(*HALO[side]), :]
        return pltpu.make_async_remote_copy(
            src_ref=src, dst_ref=halo.at[pl.ds(*HALO[BACK[side]]), :],
            send_sem=psend_sem.at[side], recv_sem=precv_sem.at[BACK[side]],
            device_id=place(side if target is None else target), device_id_type=MESH)

    def node(r, c):
        row = (r * 2 + c) * NODE
        return own[row:row + NODE, :].astype(F32)

    def put(row, value):
        part[row:row + NODE, :] = value.astype(BF16)

    w0, w1 = BLEND[0], BLEND[1]
    put(128, (w0 * w1) * (node(0, 0) + node(0, 1)))
    put(160, (w0 * w1) * (node(3, 0) + node(3, 1)))
    pl.semaphore_wait(barrier, count)
    for side in range(2, 8):
        @pl.when(present(side))
        def _():
            psf_copy(side).start()

    for side in (LEFT, RIGHT):
        n0, n1, n2, n3 = (node(r, side) for r in range(4))
        put(side * 64, (w0 * w1) * (n0 + n1) + (w0 * w0) * n2)
        put(side * 64 + NODE, (w0 * w0) * n1 + (w0 * w1) * (n2 + n3))

        @pl.when(present(side))
        def _():
            psf_copy(side).start()

    for side in range(8):
        @pl.when(jnp.logical_not(present(side)))
        def _():
            halo[pl.ds(*HALO[side]), :] = jnp.zeros((HALO[side][1], PSFW * PSFW), BF16)

    tables_in[0].wait()
    width = 512
    for t in range(INNER // width):
        if t % (chunk // width) == 0:
            image_copies[t // (chunk // width)].wait()
        sl = slice(t * width, (t + 1) * width)
        d1[:, sl] = mm(fx[...], img[:, sl].astype(BF16)).astype(BF16)

    def depth_step(ref, table, t, ylo, width_y, stride, out):
        def rhs(tile):
            sl = pl.ds(pl.multiple_of(tile * LANES, LANES), LANES)
            return jnp.concatenate([ref[:LANES, sl], ref[LANES:, sl]], axis=1)

        both = jnp.concatenate([rhs(2 * t), rhs(2 * t + 1)], axis=0)
        res = mm_t(table[...], both)
        for jj in range(2):
            for part in range(2):
                for y in range(ylo):
                    row = (part * ylo + y) * LZ
                    block = res[row:row + LZ, jj * LANES:(jj + 1) * LANES]
                    start = part * width_y + (2 * t + jj) * ylo + y
                    out[pl.ds(start, LZ, stride=stride), :] = block

    for i in range(1, len(order)):
        tables_in[i].wait()

    @pl.loop(0, 16, unroll=U_DEPTH)
    def _(t):
        depth_step(d1, gz, t, 2, PATCH, SY, spec)

    def slab(ref, t, rows, stride):
        parts = [ref[pl.ds((2 * t + h) * stride, rows), :] for h in range(2)]
        return jnp.concatenate(parts, axis=1).astype(BF16)

    @pl.loop(0, LZ // 2, unroll=U_IMAGE)
    def _(t):
        ispec[t] = mm(fy[...], slab(spec, t, 2 * PATCH, SY)).astype(BF16)

    for side in range(8):
        @pl.when(present(side))
        def _():
            psf_copy(BACK[side], side).wait_recv()
    for t in range(2):
        sl = slice(t * 512, (t + 1) * 512)
        e1[:, sl] = (mm(pown[...], own[:, sl]) + mm(phalo[...], halo[:, sl])).astype(BF16)

    @pl.loop(0, 4, unroll=U_PSF)
    def _(t):
        depth_step(e1, gzp, t, 4, PSFW, SP, pspec)

    @pl.loop(0, LZ // 2, unroll=U_BACK)
    def _(t):
        b = mm(fyp[...], slab(pspec, t, 2 * PSFW, SP)).astype(BF16)
        a = ispec[t]
        ar, ai, br, bi = a[:LXY], a[LXY:], b[:LXY], b[LXY:]
        prod = jnp.concatenate([ar * br - ai * bi, ar * bi + ai * br], axis=0)
        back = mm(gy[...], prod)
        for h in range(2):
            for part_ in range(2):
                block = back[part_ * LXY:(part_ + 1) * LXY, h * LANES:(h + 1) * LANES]
                resp[pl.ds(part_ * LZ + 2 * t + h, LXY, stride=SZ), :] = block

    def group(g):
        rows = []
        for h in range(2):
            parts = [resp[pl.ds((4 * g + 2 * h + q) * SZ, 2 * LZ), :] for q in range(2)]
            flat = jnp.concatenate(parts, axis=1).astype(BF16)
            z = mm(iz[...], flat).astype(BF16)
            for q in range(2):
                half = z[:, q * LANES:(q + 1) * LANES]
                rows.append(jnp.concatenate([half[:DEPTH], half[DEPTH:]], axis=1))
        return mm_t(ix[...], jnp.concatenate(rows, axis=0))

    for side in range(2):
        @pl.loop(0, EDGE, unroll=EDGE)
        def _(e):
            cols = pl.ds(pl.multiple_of(e * 256, 256), 256)
            ysend[side, :, cols] = group(e + side * (GROUPS - EDGE)).astype(BF16)

    def y_copy(side, target):
        dx, dy = SIDES[side]
        rows = {0: pl.ds(HALF, TILE), -1: pl.ds(0, HALF), 1: pl.ds(HALF + TILE, HALF)}[dx]
        dst = yrecv.at[BACK[side]] if dx == 0 else crecv.at[BACK[side] - 4]
        return pltpu.make_async_remote_copy(
            src_ref=ysend.at[side if dx == 0 else (dy + 1) // 2, rows, :], dst_ref=dst,
            send_sem=rsend_sem.at[side], recv_sem=rrecv_sem.at[BACK[side]],
            device_id=place(side if target is None else target), device_id_type=MESH)

    def x_copy(side, target):
        return pltpu.make_async_remote_copy(
            src_ref=xsend.at[side - 2], dst_ref=xrecv.at[BACK[side] - 2],
            send_sem=rsend_sem.at[side], recv_sem=rrecv_sem.at[BACK[side]],
            device_id=place(side if target is None else target), device_id_type=MESH)

    def response_copy(side, target=None):
        return (x_copy if side in (UP, DOWN) else y_copy)(side, target)

    for side in (UL, UR, DL, DR):
        @pl.when(present(side))
        def _():
            response_copy(side).start()

    @pl.loop(0, GROUPS - 2 * EDGE, unroll=U_INNER)
    def _(g):
        cols = pl.ds(pl.multiple_of(g * 256, 256), 256)
        value = group(g + EDGE)
        out[:, cols] = value[HALF:HALF + TILE]
        xsend[0, :, cols] = value[:HALF].astype(BF16)
        xsend[1, :, cols] = value[HALF + TILE:].astype(BF16)

    for side in (UP, DOWN, LEFT, RIGHT):
        @pl.when(present(side))
        def _():
            response_copy(side).start()

    def arrive(side, rows, cols, ref):
        @pl.when(present(side))
        def _():
            response_copy(BACK[side], side).wait_recv()
            out[rows, cols] += ref[...].astype(F32)

    top, bottom = pl.ds(0, HALF), pl.ds(TILE - HALF, HALF)
    first, last = pl.ds(0, BAND), pl.ds(INNER - BAND, BAND)
    every = pl.ds(0, TILE)
    arrive(UP, top, pl.ds(0, INNER), xrecv.at[0])
    arrive(DOWN, bottom, pl.ds(0, INNER), xrecv.at[1])
    arrive(UL, top, first, crecv.at[0])
    arrive(DL, bottom, first, crecv.at[2])
    arrive(LEFT, every, first, yrecv.at[0])
    arrive(UR, top, last, crecv.at[1])
    arrive(DR, bottom, last, crecv.at[3])
    arrive(RIGHT, every, last, yrecv.at[1])
    for side in range(8):
        @pl.when(present(side))
        def _():
            psf_copy(side).wait_send()
            response_copy(side).wait_send()


def compute(image, psfs, *consts):
    vmem, anywhere = pl.BlockSpec(memory_space=pltpu.VMEM), pl.BlockSpec(memory_space=pltpu.HBM)
    dma = pltpu.SemaphoreType.DMA
    return pl.pallas_call(
        kernel,
        out_shape=jax.ShapeDtypeStruct((TILE, INNER), F32),
        in_specs=[anywhere] * (2 + len(consts)),
        out_specs=vmem,
        scratch_shapes=[
            pltpu.VMEM((TILE, INNER), F32),
            pltpu.VMEM((8 * PSFW, PSFW * PSFW), BF16),
            pltpu.VMEM((6 * PSFW, PSFW * PSFW), BF16),
            pltpu.VMEM((10 * PSFW, PSFW * PSFW), BF16),
            pltpu.VMEM((2 * LANES, INNER), BF16),
            pltpu.VMEM((2 * LANES, PSFW * PSFW), BF16),
            pltpu.VMEM((LZ * SY, LANES), F32),
            pltpu.VMEM((LZ * SP, LANES), F32),
            pltpu.VMEM((LZ // 2, 2 * LXY, 2 * LANES), BF16),
            pltpu.VMEM((LXY * SZ, LANES), F32),
            pltpu.VMEM((2, EXT, BAND), BF16),
            pltpu.VMEM((2, HALF, INNER), BF16),
            pltpu.VMEM((2, TILE, BAND), BF16),
            pltpu.VMEM((2, HALF, INNER), BF16),
            pltpu.VMEM((4, HALF, BAND), BF16),
            *[pltpu.VMEM(c.shape, BF16) for c in consts],
            dma((4,)), dma, dma((len(consts),)), dma((8,)), dma((8,)), dma((8,)), dma((8,)),
        ],
        compiler_params=pltpu.CompilerParams(
            vmem_limit_bytes=40 * 1024 * 1024, collective_id=0, has_side_effects=True),
    )(*[pltpu.with_memory_space_constraint(v, pltpu.HBM) for v in (image, psfs.reshape(8 * PSFW, PSFW * PSFW), *consts)])


def body(image, psfs):
    return compute(image, psfs, *tables())


def solution(mesh):
    placed = (P("gx", "gy"), P("gx", "gy", None, None))
    return jax.shard_map(body, mesh=mesh, in_specs=placed, out_specs=P("gx", "gy"), check_vma=False)
```
